128 devices in a mesh: src: 8 (over z, core), tgt: 16 (over x, y).
Axes of the slice: x: 4, y: 4, z: 4, core: 2. Of those that a mesh axis runs over, the one named last changes fastest.
Arguments:
- src_points: bfloat16 [64, 256, 128], P('src', 'tgt')
- tgt_points: bfloat16 [128, 256, 128], P('tgt', 'src'), may hold values from -1.5 to 1.5
- src_mass: bfloat16 [64, 256], P('src', 'tgt'), may hold values from 0.099609375 to 10
- tgt_mass: bfloat16 [128, 256], P('tgt', 'src'), may hold values from 0.099609375 to 10
- src_potential: bfloat16 [64, 256], P('src', 'tgt'), may hold values from -452 to 452
- tgt_potential: bfloat16 [128, 256], P('tgt', 'src'), may hold values from -452 to 452
- src_counts: int32 [64], P('src'), may hold values from 16 to 256, as said below
- tgt_counts: int32 [128], P('tgt'), may hold values from 16 to 256, as said below
- keep: int32 [64, 128], P('src', 'tgt'), may hold values from 0 to 1, as said below
Outputs:
- images: float32 [64, 256, 128], P('src', 'tgt')
- src_final: float32 [64, 256], P('src', 'tgt')
- tgt_final: float32 [128, 256], P('tgt', 'src')
The draws below stay inside these ranges and needn't reach their ends.
Inputs may be any that keep to these rules, and one draw needn't show every extreme that they name: `keep`: every source block keeps at least one target block and every target block is kept by at least one source block. `src_counts`: some source block is full. `tgt_counts`: some target block is full.
All inputs are finite; a program needn't handle non-finite values.
Results may differ from the reference program's by a relative error of at most 0.0003.
Values may be sent and summed in bfloat16 or wider, within the bound.
A program may use at most 64 MiB of HBM per device.

```python
import math
import jax
import jax.numpy as jnp
from jax import lax

W = 128
BLOCK = 256
ITERS = 4
NSB = 64
NTB = 128


def draw_src_points(key, part):
    values = 0.25 * jax.random.normal(key, (NSB, BLOCK, W), jnp.float32)
    return values.astype(jnp.bfloat16)


def coarse_potential(key, rows):
    rough = jnp.clip(jax.random.normal(jax.random.fold_in(key, 22), (rows, BLOCK), jnp.float32), -2.0, 2.0)
    offset = jnp.clip(150.0 * jax.random.normal(jax.random.fold_in(key, 21), (rows, BLOCK), jnp.float32), -450.0, 450.0)
    return (offset + rough).astype(jnp.bfloat16)


def draw_src_potential(key, part):
    return coarse_potential(jax.random.fold_in(key, 31), NSB)


def draw_tgt_potential(key, part):
    return coarse_potential(jax.random.fold_in(key, 37), NTB)


def live_counts(key, total):
    lowest = max(1, BLOCK // 16)
    values = jax.random.randint(key, (total,), lowest, BLOCK + 1)
    order = jax.random.permutation(jax.random.fold_in(key, 7), total)
    values = values.at[order[0]].set(BLOCK)
    values = values.at[order[1]].set(lowest)
    return values.astype(jnp.int32)


def draw_src_counts(key, part):
    return live_counts(jax.random.fold_in(key, 11), NSB)


def draw_tgt_counts(key, part):
    return live_counts(jax.random.fold_in(key, 13), NTB)


def draw_keep(key, part):
    rates = jax.random.randint(jax.random.fold_in(key, 1), (NSB, 1), 1, 9)
    rolls = jax.random.randint(jax.random.fold_in(key, 2), (NSB, NTB), 0, 24)
    shift_a = jax.random.randint(jax.random.fold_in(key, 3), (), 0, NTB)
    shift_b = jax.random.randint(jax.random.fold_in(key, 4), (), 0, NSB)
    rows = jnp.arange(NSB, dtype=jnp.int32)[:, None]
    cols = jnp.arange(NTB, dtype=jnp.int32)[None, :]
    cover_a = cols == (rows * NTB // NSB + shift_a) % NTB
    cover_b = rows == (cols * NSB // NTB + shift_b) % NSB
    return ((rolls < rates) | cover_a | cover_b).astype(jnp.int32)


def levels(rng, extent, pieces, smallest, largest):
    loudness = 1.0
    for position, shards_of in pieces:
        heights = jax.random.uniform(jax.random.fold_in(jax.random.fold_in(rng, 6), position), (shards_of,), jnp.float32, smallest / len(pieces), largest / len(pieces))
        loudness = loudness * jnp.repeat(jnp.exp(heights), extent[position] // shards_of).reshape((-1,) + (1,) * (len(extent) - 1 - position))
    return loudness


def centred(own_key, shape, scale, most, split=(), kind=jnp.bfloat16):
    array = scale * jax.random.normal(own_key, shape, jnp.float32)
    if split:
        array = array * levels(own_key, shape, split, -0.22, 0.18)
    return jnp.clip(array, -most, most).astype(kind)


def setup_inputs(seed: int = 0) -> dict:
    keys = jax.random.split(jax.random.key(seed), 10)
    src_points = draw_src_points(jax.random.fold_in(keys[9], 71), 0)
    tgt_points = centred(keys[1], (NTB, BLOCK, W), 0.25, 1.5, ((0, 16), (1, 8)))
    src_mass = jnp.clip(jnp.exp(math.log(10.0) - 4.609084 * jax.random.uniform(keys[2], (NSB, BLOCK), jnp.float32) ** levels(keys[2], (NSB, BLOCK), ((0, 8), (1, 16)), -0.2, 0.2)), 0.099609375, 10.0).astype(jnp.bfloat16)
    tgt_mass = jnp.clip(jnp.exp(math.log(10.0) - 4.609084 * jax.random.uniform(keys[3], (NTB, BLOCK), jnp.float32) ** levels(keys[3], (NTB, BLOCK), ((0, 16), (1, 8)), -0.2, 0.2)), 0.099609375, 10.0).astype(jnp.bfloat16)
    src_potential = draw_src_potential(jax.random.fold_in(keys[9], 71), 0)
    tgt_potential = draw_tgt_potential(jax.random.fold_in(keys[9], 71), 0)
    src_counts = draw_src_counts(jax.random.fold_in(keys[9], 71), 0)
    tgt_counts = draw_tgt_counts(jax.random.fold_in(keys[9], 71), 0)
    keep = draw_keep(jax.random.fold_in(keys[9], 71), 0)
    return {"src_points": src_points, "tgt_points": tgt_points, "src_mass": src_mass, "tgt_mass": tgt_mass, "src_potential": src_potential, "tgt_potential": tgt_potential, "src_counts": src_counts, "tgt_counts": tgt_counts, "keep": keep}


EPSILON = 0.1
FLOOR = -1.0e30


def reference(src_points, tgt_points, src_mass, tgt_mass, src_potential, tgt_potential, src_counts, tgt_counts, keep):
    nsb, blk, width = src_points.shape
    ntb = tgt_points.shape[0]
    xs = src_points.astype(jnp.float32)
    ys = tgt_points.astype(jnp.float32).reshape(ntb * blk, width)
    y_half = 0.5 * jnp.sum(ys * ys, axis=1)
    slots = jnp.arange(blk, dtype=jnp.int32)
    src_live = slots[None, :] < src_counts[:, None]
    tgt_live = (slots[None, :] < tgt_counts[:, None]).reshape(-1)
    log_a = jnp.log(src_mass.astype(jnp.float32))
    log_b = jnp.log(tgt_mass.astype(jnp.float32)).reshape(-1)
    kept = jnp.repeat(keep > 0, blk, axis=1)

    def tile(x):
        x_half = 0.5 * jnp.sum(x * x, axis=1)
        return x_half[:, None] + y_half[None, :] - jnp.dot(x, ys.T, precision=lax.Precision.HIGHEST)

    def sweep(f_now, g_now):
        def visit(carry, item):
            colmax, colsum = carry
            x, live, lga, fpart, pair = item
            cost = tile(x)
            row_ok = pair[None, :] & tgt_live[None, :]
            col_ok = pair[None, :] & live[:, None]
            scored = jnp.where(row_ok, log_b[None, :] + (g_now[None, :] - cost) / EPSILON, FLOOR)
            rmax = jnp.max(scored, axis=1)
            rsum = jnp.sum(jnp.where(row_ok, jnp.exp(scored - rmax[:, None]), 0.0), axis=1)
            colterm = jnp.where(col_ok, lga[:, None] + (fpart[:, None] - cost) / EPSILON, FLOOR)
            peak = jnp.maximum(colmax, jnp.max(colterm, axis=0))
            colsum = colsum * jnp.exp(colmax - peak) + jnp.sum(jnp.where(col_ok, jnp.exp(colterm - peak[None, :]), 0.0), axis=0)
            return (peak, colsum), -EPSILON * (rmax + jnp.log(rsum))

        start = (jnp.full((ntb * blk,), FLOOR, jnp.float32), jnp.zeros((ntb * blk,), jnp.float32))
        (colmax, colsum), f_new = lax.scan(visit, start, (xs, src_live, log_a, f_now, kept))
        return f_new, -EPSILON * (colmax + jnp.log(colsum))

    f_cur = src_potential.astype(jnp.float32)
    g_cur = tgt_potential.astype(jnp.float32).reshape(-1)
    for step in range(ITERS):
        f_new, g_new = sweep(f_cur, g_cur)
        f_cur = 0.5 * (f_cur + f_new)
        g_cur = 0.5 * (g_cur + g_new)

    def project(carry, item):
        x, pair = item
        cost = tile(x)
        row_ok = pair[None, :] & tgt_live[None, :]
        scored = jnp.where(row_ok, log_b[None, :] + (g_cur[None, :] - cost) / EPSILON, FLOOR)
        rmax = jnp.max(scored, axis=1)
        weights = jnp.where(row_ok, jnp.exp(scored - rmax[:, None]), 0.0)
        total = jnp.sum(weights, axis=1)
        moved = jnp.dot(weights, ys, precision=lax.Precision.HIGHEST) / total[:, None]
        return carry, moved

    unused, images = lax.scan(project, jnp.zeros((), jnp.float32), (xs, kept))
    return images, f_cur, g_cur.reshape(ntb, blk)
```

```python
import math

import jax
import jax.numpy as jnp
from jax import lax
from jax.experimental import pallas as pl
from jax.experimental.pallas import tpu as pltpu
from jax.sharding import PartitionSpec as P

ITERS = 4
EPSILON = 0.1
NEG = -1e30
SCALE = math.log2(math.e) / EPSILON
MESH = pl.DeviceIdType.MESH

NT, NS = 16, 8
PTS = 2048
TILES = 16
FAR_T = sorted(range(1, NT), key=lambda d: -(min(d // 4, 4 - d // 4) + min(d % 4, 4 - d % 4)))
FAR_S = sorted(range(1, NS), key=lambda d: -(2 * min(d // 2, 4 - d // 2) + d % 2))


def iota(shape, dim):
    return lax.broadcasted_iota(jnp.int32, shape, dim)


def tree(op, parts):
    parts = list(parts)
    while len(parts) > 1:
        parts = [op(parts[i], parts[i + 1]) if i + 1 < len(parts) else parts[i] for i in range(0, len(parts), 2)]
    return parts[0]


def fold(op, block):
    return tree(op, [block[8 * i : 8 * i + 8, :] for i in range(block.shape[0] // 8)])


def to_lanes(block):
    n = block.shape[1]
    put = (iota((n, 8 * n), 1) % n == iota((n, 8 * n), 0)).astype(jnp.bfloat16)
    wide = jnp.dot(block, put, preferred_element_type=jnp.float32)
    own = iota((8, 8 * n), 1) // n == iota((8, 8 * n), 0)
    return jnp.sum(jnp.where(own, wide, 0.0), axis=0, keepdims=True)


def half_norm(points):
    wide = points.astype(jnp.float32)
    square = wide * wide
    high = square.astype(jnp.bfloat16)
    low = (square - high.astype(jnp.float32)).astype(jnp.bfloat16)
    ones = jnp.ones((8, 128), jnp.bfloat16)
    dims = (((1,), (1,)), ((), ()))
    total = lax.dot_general(ones, high, dims, preferred_element_type=jnp.float32) + lax.dot_general(
        ones, low, dims, preferred_element_type=jnp.float32
    )
    return 0.5 * total[0:1, :]


def kernel(
    scnt, tcnt, keep, x_in, y_in, a_in, b_in, f_in, g_in, img_out, f_out, g_out,
    xs, ys, sp, tp, ytr, cmat, rmat, vbuf, fb, gb, pn, pt, whi, wlo, fl, gl,
    rsend, rrecv, csend, crecv, msg, mrecv,
    xsem, spsem, ysem, tpsem, rsem, csem, msem,
):
    src = lax.axis_index("src")
    tgt = lax.axis_index("tgt")
    sz, sc = lax.div(src, 2), lax.rem(src, 2)
    tx, ty = lax.div(tgt, 4), lax.rem(tgt, 4)

    def tpeer(d):
        return lax.rem(tx + d // 4, 4) * 4 + lax.rem(ty + d % 4, 4)

    def speer(d):
        return lax.rem(sz + d // 2, 4) * 2 + lax.rem(sc + d % 2, 2)

    barrier = pltpu.get_barrier_semaphore()
    for d in FAR_T:
        pl.semaphore_signal(barrier, inc=1, device_id={"tgt": tpeer(d)}, device_id_type=MESH)
    for d in FAR_S:
        pl.semaphore_signal(barrier, inc=1, device_id={"src": speer(d)}, device_id_type=MESH)

    def push(source, dest, sem, device):
        pltpu.make_async_remote_copy(
            src_ref=source, dst_ref=dest, send_sem=sem.at[0], recv_sem=sem.at[1], device_id=device, device_id_type=MESH
        ).start()

    def done(ref, sem):
        pltpu.make_async_copy(ref, ref, sem).wait()

    lane = iota((1, 128), 1)
    xs[pl.ds(tgt, 1)] = x_in[...].reshape(1, 128, 128)
    ys[pl.ds(src * 2, 2)] = y_in[...].reshape(2, 128, 128)
    fl[...] = jnp.zeros((8, 128), jnp.float32)
    gl[...] = jnp.zeros((2, 8, 128), jnp.float32)
    fl[0:1, :] = to_lanes(f_in[...])
    fl[1:2, :] = jnp.log2(to_lanes(a_in[...]))
    fl[2:3, :] = half_norm(x_in[...])
    tgt_rows = (to_lanes(g_in[...]), jnp.log2(to_lanes(b_in[...])), half_norm(y_in[...].reshape(256, 128)))
    for r, row in enumerate(tgt_rows):
        for h in range(2):
            gl[h, r : r + 1, :] = row[:, 128 * h : 128 * h + 128]
    sp[pl.ds(tgt, 1)] = fl[...].reshape(1, 8, 128)
    tp[pl.ds(src * 2, 2)] = gl[...]

    pl.semaphore_wait(barrier, len(FAR_T) + len(FAR_S))
    for d in FAR_T:
        push(x_in, xs.at[tgt], xsem, {"tgt": tpeer(d)})
    for d in FAR_S:
        push(y_in, ys.at[pl.ds(src * 2, 2)], ysem, {"src": speer(d)})
    for d in FAR_T:
        push(fl, sp.at[tgt], spsem, {"tgt": tpeer(d)})
    for d in FAR_S:
        push(gl, tp.at[pl.ds(src * 2, 2)], tpsem, {"src": speer(d)})

    for p in range(8):
        for par in range(2):
            row = jnp.zeros((1, 128), jnp.float32)
            for q in range(4):
                pen = jnp.where(keep[p, par * 4 + q] > 0, 0.0, NEG)
                row = jnp.where(lane // 32 == q, pen, row)
            pn[par, pl.ds(16 * p, 16), :] = jnp.broadcast_to(row, (16, 128))
    for q in range(8):
        row = jnp.zeros((1, 128), jnp.float32)
        for p in range(8):
            pen = jnp.where(keep[p, q] > 0, 0.0, NEG)
            row = jnp.where(lane // 16 == p, pen, row)
        pt[pl.ds(32 * q, 32), :] = jnp.broadcast_to(row, (32, 128))
    r16, l16 = iota((16, 128), 0), iota((16, 128), 1)
    sdead = jnp.zeros((16, 128), jnp.float32)
    tdead = jnp.zeros((16, 128), jnp.float32)
    for p in range(8):
        sdead = jnp.where((l16 // 16 == p) & (r16 * 16 + l16 % 16 >= scnt[p]), NEG, sdead)
        tdead = jnp.where(((r16 % 2) * 4 + l16 // 32 == p) & ((r16 // 2) * 32 + l16 % 32 >= tcnt[p]), NEG, tdead)
    eye = iota((128, 128), 0) == iota((128, 128), 1)

    def spread(rows, dest):
        for t in range(TILES):
            diag = jnp.where(eye, jnp.broadcast_to(rows[t : t + 1, :], (128, 128)), 0.0)
            column = jnp.sum(diag, axis=1, keepdims=True)
            dest[pl.ds(128 * t, 128), :] = jnp.broadcast_to(column, (128, 128))

    def score(mat, points, others, penalty, span):
        def pair(c, carry):
            two = points[pl.ds(2 * c, 2)].reshape(256, 128)
            for r in range(8):
                part = others[2 * r : 2 * r + 2].reshape(256, 128)
                prod = lax.dot_general(part, two, (((1,), (1,)), ((), ())), preferred_element_type=jnp.float32)
                for h in range(2):
                    mat[2 * c + h, pl.ds(256 * r, 256), :] = SCALE * prod[:, 128 * h : 128 * h + 128] + penalty(h)
            return carry

        lax.fori_loop(0, TILES // 2, pair, 0)

    def weigh(mat, c, col, slot):
        tops = []
        for r in range(16):
            v = mat[c, pl.ds(128 * r, 128), :] + col[pl.ds(128 * r, 128), :]
            vbuf[slot, pl.ds(128 * r, 128), :] = v
            tops.append(fold(jnp.maximum, v))
        return jnp.max(tree(jnp.maximum, tops), axis=0, keepdims=True)

    def lse(mat, col, out):
        def step(i, carry):
            for h in range(2):
                c = 2 * i + h
                top = weigh(mat, c, col, h)
                sums = []
                for r in range(16):
                    sums.append(fold(jnp.add, jnp.exp2(vbuf[h, pl.ds(128 * r, 128), :] - top)))
                total = jnp.sum(tree(jnp.add, sums), axis=0, keepdims=True)
                out[pl.ds(c, 1), :] = top + jnp.log2(total)
            return carry

        lax.fori_loop(0, TILES // 2, step, 0)

    def merge(ref, k):
        top = tree(jnp.maximum, [ref[k, i] for i in range(ref.shape[1])])
        total = tree(jnp.add, [jnp.exp2(ref[k, i] - top) for i in range(ref.shape[1])])
        return top + jnp.log2(total)

    done(ys.at[pl.ds(0, 14)], ysem.at[1])
    done(tp.at[pl.ds(0, 14)], tpsem.at[1])
    done(xs.at[pl.ds(0, 15)], xsem.at[1])
    done(sp.at[pl.ds(0, 15)], spsem.at[1])

    def rows_of(ref, r):
        return jnp.concatenate([ref[t, r : r + 1, :] for t in range(TILES)], axis=0)

    f, la, xh = rows_of(sp, 0), rows_of(sp, 1), rows_of(sp, 2)
    g, lb, yh = rows_of(tp, 0), rows_of(tp, 1), rows_of(tp, 2)
    la = la + sdead
    lb = lb + tdead
    spread(lb + SCALE * (g - yh), gb)
    spread(la + SCALE * (f - xh), fb)
    score(rmat, xs, ys, lambda h: pt[...], 256)

    def send_rows(k):
        rrecv[k, pl.ds(tgt, 1)] = rsend[k].reshape(1, 16, 128)
        for d in FAR_T:
            push(rsend.at[k], rrecv.at[k, tgt], rsem.at[k], {"tgt": tpeer(d)})

    def send_cols(k):
        crecv[k, pl.ds(src, 1)] = csend[k].reshape(1, 16, 128)
        for d in FAR_S:
            push(csend.at[k], crecv.at[k, src], csem.at[k], {"src": speer(d)})

    def take_rows(k, f):
        done(rrecv.at[k, pl.ds(0, 15)], rsem.at[k, 1])
        f = 0.5 * (f + (xh - merge(rrecv, k) * (1.0 / SCALE)))
        return f

    def take_cols(k, g):
        done(crecv.at[k, pl.ds(0, 7)], csem.at[k, 1])
        g = 0.5 * (g + (yh - merge(crecv, k) * (1.0 / SCALE)))
        return g

    lse(rmat, gb, rsend.at[0])
    send_rows(0)
    score(cmat, ys, xs, lambda h: jnp.concatenate([pn[h], pn[h]], axis=0), 256)
    for t in range(TILES):
        ytr[:, pl.ds(128 * t, 128)] = jnp.transpose(ys[t].astype(jnp.float32)).astype(jnp.bfloat16)
    lse(cmat, fb, csend.at[0])
    send_cols(0)
    for k in range(1, ITERS):
        if k % 2:
            f = take_rows(k - 1, f)
            spread(la + SCALE * (f - xh), fb)
            lse(cmat, fb, csend.at[k])
            send_cols(k)
            g = take_cols(k - 1, g)
            spread(lb + SCALE * (g - yh), gb)
            lse(rmat, gb, rsend.at[k])
            send_rows(k)
        else:
            g = take_cols(k - 1, g)
            spread(lb + SCALE * (g - yh), gb)
            lse(rmat, gb, rsend.at[k])
            send_rows(k)
            f = take_rows(k - 1, f)
            spread(la + SCALE * (f - xh), fb)
            lse(cmat, fb, csend.at[k])
            send_cols(k)
    g = take_cols(ITERS - 1, g)
    spread(lb + SCALE * (g - yh), gb)

    def project(i, carry):
        d = 15 - i
        c = lax.rem(tx + lax.div(d, 4), 4) * 4 + lax.rem(ty + lax.rem(d, 4), 4)
        top = weigh(rmat, c, gb, 0)
        sums = []
        for r in range(16):
            w = jnp.exp2(vbuf[0, pl.ds(128 * r, 128), :] - top)
            high = w.astype(jnp.bfloat16)
            whi[pl.ds(128 * r, 128), :] = high
            wlo[pl.ds(128 * r, 128), :] = (w - high.astype(jnp.float32)).astype(jnp.bfloat16)
            sums.append(fold(jnp.add, w))
        total = jnp.sum(tree(jnp.add, sums), axis=0, keepdims=True)
        moved = jnp.dot(ytr[...], whi[...], preferred_element_type=jnp.float32) + jnp.dot(
            ytr[...], wlo[...], preferred_element_type=jnp.float32
        )
        msg[d, 0:128, :] = moved
        r8 = iota((8, 128), 0)
        msg[d, 128:136, :] = jnp.where(r8 == 0, top, jnp.where(r8 == 1, total, 0.0))

        @pl.when(d > 0)
        def _():
            push(msg.at[d], mrecv.at[d], msem, {"tgt": c})

        return carry

    lax.fori_loop(0, 16, project, 0)
    f = take_rows(ITERS - 1, f)
    fb[0:16, :] = f
    f_out[...] = fb[pl.ds(tgt, 1), :]
    gb[0:16, :] = g
    g_out[...] = gb[pl.ds(src * 2, 2), :]
    mrecv[0] = msg[0]
    done(mrecv.at[pl.ds(1, 15)], msem.at[1])
    tops = [mrecv[d, 128:129, :] for d in range(16)]
    top = tree(jnp.maximum, tops)
    scales = [jnp.exp2(t - top) for t in tops]
    total = tree(jnp.add, [scales[d] * mrecv[d, 129:130, :] for d in range(16)])
    inv = 1.0 / total
    moved = scales[0] * mrecv[0, 0:128, :]
    for d in range(1, 16):
        moved = moved + scales[d] * mrecv[d, 0:128, :]
    img_out[...] = jnp.transpose(moved * inv)

    done(xs.at[pl.ds(0, 15)], xsem.at[0])
    done(sp.at[pl.ds(0, 15)], spsem.at[0])
    done(ys.at[pl.ds(0, 14)], ysem.at[0])
    done(tp.at[pl.ds(0, 14)], tpsem.at[0])
    for k in range(ITERS):
        done(rrecv.at[k, pl.ds(0, 15)], rsem.at[k, 0])
        done(crecv.at[k, pl.ds(0, 7)], csem.at[k, 0])
    done(mrecv.at[pl.ds(1, 15)], msem.at[0])


def on_device(src_points, tgt_points, src_mass, tgt_mass, src_potential, tgt_potential, src_counts, tgt_counts, keep):
    f32, bf16 = jnp.float32, jnp.bfloat16
    vmem = pl.BlockSpec(memory_space=pltpu.VMEM)
    smem = pl.BlockSpec(memory_space=pltpu.SMEM)
    dma = pltpu.SemaphoreType.DMA
    images, f, g = pl.pallas_call(
        kernel,
        out_shape=(
            jax.ShapeDtypeStruct((128, 128), f32),
            jax.ShapeDtypeStruct((1, 128), f32),
            jax.ShapeDtypeStruct((2, 128), f32),
        ),
        in_specs=[smem] * 3 + [vmem] * 6,
        out_specs=(vmem, vmem, vmem),
        scratch_shapes=[
            pltpu.VMEM((16, 128, 128), bf16),
            pltpu.VMEM((16, 128, 128), bf16),
            pltpu.VMEM((16, 8, 128), f32),
            pltpu.VMEM((16, 8, 128), f32),
            pltpu.VMEM((128, PTS), bf16),
            pltpu.VMEM((16, PTS, 128), f32),
            pltpu.VMEM((16, PTS, 128), f32),
            pltpu.VMEM((2, PTS, 128), f32),
            pltpu.VMEM((PTS, 128), f32),
            pltpu.VMEM((PTS, 128), f32),
            pltpu.VMEM((2, 128, 128), f32),
            pltpu.VMEM((256, 128), f32),
            pltpu.VMEM((PTS, 128), bf16),
            pltpu.VMEM((PTS, 128), bf16),
            pltpu.VMEM((8, 128), f32),
            pltpu.VMEM((2, 8, 128), f32),
            pltpu.VMEM((ITERS, 16, 128), f32),
            pltpu.VMEM((ITERS, 16, 16, 128), f32),
            pltpu.VMEM((ITERS, 16, 128), f32),
            pltpu.VMEM((ITERS, 8, 16, 128), f32),
            pltpu.VMEM((16, 136, 128), f32),
            pltpu.VMEM((16, 136, 128), f32),
            dma((2,)),
            dma((2,)),
            dma((2,)),
            dma((2,)),
            dma((ITERS, 2)),
            dma((ITERS, 2)),
            dma((2,)),
        ],
        compiler_params=pltpu.CompilerParams(
            collective_id=0, has_side_effects=True, vmem_limit_bytes=60 * 1024 * 1024
        ),
        name="sinkhorn",
    )(
        src_counts,
        tgt_counts,
        keep,
        src_points.reshape(128, 128),
        tgt_points.reshape(2, 128, 128),
        src_mass,
        tgt_mass,
        src_potential,
        tgt_potential,
    )
    return images.reshape(8, 16, 128), f.reshape(8, 16), g.reshape(8, 32)


def solution(mesh):
    return jax.shard_map(
        on_device,
        mesh=mesh,
        in_specs=(
            P("src", "tgt", None),
            P("tgt", "src", None),
            P("src", "tgt"),
            P("tgt", "src"),
            P("src", "tgt"),
            P("tgt", "src"),
            P("src"),
            P("tgt"),
            P("src", "tgt"),
        ),
        out_specs=(P("src", "tgt", None), P("src", "tgt"), P("tgt", "src")),
        check_vma=False,
    )
```

```python
import math

import jax
import jax.numpy as jnp
from jax import lax
from jax.experimental import pallas as pl
from jax.experimental.pallas import tpu as pltpu
from jax.sharding import PartitionSpec as P

ITERS = 4
EPSILON = 0.1
NEG = -1e30
SCALE = math.log2(math.e) / EPSILON
MESH = pl.DeviceIdType.MESH

NT, NS = 16, 8
PTS = 2048
TILES = 16
WIDE = 4
FAR_T = sorted(range(1, NT), key=lambda d: -(min(d // 4, 4 - d // 4) + min(d % 4, 4 - d % 4)))
LINE = (1, 3, 2)
FAR_S = sorted(range(1, NS), key=lambda d: -(2 * min(d // 2, 4 - d // 2) + d % 2))


def iota(shape, dim):
    return lax.broadcasted_iota(jnp.int32, shape, dim)


def tree(op, parts):
    parts = list(parts)
    while len(parts) > 1:
        parts = [op(parts[i], parts[i + 1]) if i + 1 < len(parts) else parts[i] for i in range(0, len(parts), 2)]
    return parts[0]


def fold(op, block):
    return tree(op, [block[8 * i : 8 * i + 8, :] for i in range(block.shape[0] // 8)])


def to_lanes(block):
    n = block.shape[1]
    put = (iota((n, 8 * n), 1) % n == iota((n, 8 * n), 0)).astype(jnp.bfloat16)
    wide = jnp.dot(block, put, preferred_element_type=jnp.float32)
    own = iota((8, 8 * n), 1) // n == iota((8, 8 * n), 0)
    return jnp.sum(jnp.where(own, wide, 0.0), axis=0, keepdims=True)


def from_lanes(rows, n):
    per = 128 // n
    home, lane = iota((8, 128), 0), iota((8, 128), 1)
    wide = jnp.zeros((8, 128), jnp.float32)
    for h in range(rows.shape[0]):
        wide = jnp.where(home == h * per + lane // n, jnp.broadcast_to(rows[h : h + 1, :], (8, 128)), wide)
    put = (iota((128, n), 0) % n == iota((128, n), 1)).astype(jnp.bfloat16)
    high = wide.astype(jnp.bfloat16)
    rest = wide - high.astype(jnp.float32)
    mid = rest.astype(jnp.bfloat16)
    low = (rest - mid.astype(jnp.float32)).astype(jnp.bfloat16)
    parts = [jnp.dot(part, put, preferred_element_type=jnp.float32) for part in (high, mid, low)]
    return parts[0] + parts[1] + parts[2]


def half_norm(points):
    wide = points.astype(jnp.float32)
    square = wide * wide
    high = square.astype(jnp.bfloat16)
    low = (square - high.astype(jnp.float32)).astype(jnp.bfloat16)
    ones = jnp.ones((8, 128), jnp.bfloat16)
    dims = (((1,), (1,)), ((), ()))
    total = lax.dot_general(ones, high, dims, preferred_element_type=jnp.float32) + lax.dot_general(
        ones, low, dims, preferred_element_type=jnp.float32
    )
    return 0.5 * total[0:1, :]


def kernel(
    scnt, tcnt, keep, x_in, y_in, a_in, b_in, f_in, g_in, img_out, f_out, g_out,
    xs, ys, sp, tp, ytr, cmat, rmat, vbuf, fb, gb, pn, pt, whi, wlo, fl, gl,
    rsend, rrecv, csend, crecv, msg, mrecv,
    xsem, spsem, ysem, tpsem, rsem, csem, msem,
):
    src = lax.axis_index("src")
    tgt = lax.axis_index("tgt")
    sz, sc = lax.div(src, 2), lax.rem(src, 2)
    tx, ty = lax.div(tgt, 4), lax.rem(tgt, 4)

    def tpeer(d):
        return lax.rem(tx + d // 4, 4) * 4 + lax.rem(ty + d % 4, 4)

    def speer(d):
        return lax.rem(sz + d // 2, 4) * 2 + lax.rem(sc + d % 2, 2)

    barrier = pltpu.get_barrier_semaphore()
    for d in FAR_T:
        pl.semaphore_signal(barrier, inc=1, device_id={"tgt": tpeer(d)}, device_id_type=MESH)
    for d in FAR_S:
        pl.semaphore_signal(barrier, inc=1, device_id={"src": speer(d)}, device_id_type=MESH)

    def push(source, dest, sem, device):
        pltpu.make_async_remote_copy(
            src_ref=source, dst_ref=dest, send_sem=sem.at[0], recv_sem=sem.at[1], device_id=device, device_id_type=MESH
        ).start()

    def done(ref, sem):
        pltpu.make_async_copy(ref, ref, sem).wait()

    lane = iota((1, 128), 1)
    xs[pl.ds(tgt, 1)] = x_in[...].reshape(1, 128, 128)
    ys[pl.ds(src * 2, 2)] = y_in[...].reshape(2, 128, 128)
    fl[...] = jnp.zeros((8, 128), jnp.float32)
    gl[...] = jnp.zeros((2, 8, 128), jnp.float32)
    fl[0:1, :] = to_lanes(f_in[...])
    fl[1:2, :] = jnp.log2(to_lanes(a_in[...]))
    fl[2:3, :] = half_norm(x_in[...])
    tgt_rows = (to_lanes(g_in[...]), jnp.log2(to_lanes(b_in[...])), half_norm(y_in[...].reshape(256, 128)))
    for r, row in enumerate(tgt_rows):
        for h in range(2):
            gl[h, r : r + 1, :] = row[:, 128 * h : 128 * h + 128]
    sp[pl.ds(tgt, 1)] = fl[...].reshape(1, 8, 128)
    tp[pl.ds(src * 2, 2)] = gl[...]

    pl.semaphore_wait(barrier, len(FAR_T) + len(FAR_S))
    for i, n in enumerate(LINE):
        push(x_in, xs.at[tgt], xsem.at[i], {"tgt": tpeer(4 * n)})
        push(x_in, xs.at[tgt], xsem.at[3 + i], {"tgt": tpeer(n)})
        push(y_in, ys.at[pl.ds(src * 2, 2)], ysem.at[i], {"src": speer(2 * n)})
    push(y_in, ys.at[pl.ds(src * 2, 2)], ysem.at[3], {"src": speer(1)})
    for d in FAR_T:
        push(fl, sp.at[tgt], spsem, {"tgt": tpeer(d)})
    for d in FAR_S:
        push(gl, tp.at[pl.ds(src * 2, 2)], tpsem, {"src": speer(d)})

    for p in range(8):
        for par in range(2):
            row = jnp.zeros((1, 128), jnp.float32)
            for q in range(4):
                pen = jnp.where(keep[p, par * 4 + q] > 0, 0.0, NEG)
                row = jnp.where(lane // 32 == q, pen, row)
            pn[par, pl.ds(16 * p, 16), :] = jnp.broadcast_to(row, (16, 128))
    for q in range(8):
        row = jnp.zeros((1, 128), jnp.float32)
        for p in range(8):
            pen = jnp.where(keep[p, q] > 0, 0.0, NEG)
            row = jnp.where(lane // 16 == p, pen, row)
        pt[pl.ds(32 * q, 32), :] = jnp.broadcast_to(row, (32, 128))
    r16, l16 = iota((16, 128), 0), iota((16, 128), 1)
    sdead = jnp.zeros((16, 128), jnp.float32)
    tdead = jnp.zeros((16, 128), jnp.float32)
    for p in range(8):
        sdead = jnp.where((l16 // 16 == p) & (r16 * 16 + l16 % 16 >= scnt[p]), NEG, sdead)
        tdead = jnp.where(((r16 % 2) * 4 + l16 // 32 == p) & ((r16 // 2) * 32 + l16 % 32 >= tcnt[p]), NEG, tdead)
    eye = iota((128, 128), 0) == iota((128, 128), 1)

    def spread(rows, dest):
        for t in range(TILES):
            diag = jnp.where(eye, jnp.broadcast_to(rows[t : t + 1, :], (128, 128)), 0.0)
            column = jnp.sum(diag, axis=1, keepdims=True)
            dest[pl.ds(128 * t, 128), :] = jnp.broadcast_to(column, (128, 128))

    def score(mat, points, others, penalty, span):
        def pair(c, carry):
            two = points[pl.ds(2 * c, 2)].reshape(256, 128)
            for r in range(8):
                part = others[2 * r : 2 * r + 2].reshape(256, 128)
                prod = lax.dot_general(part, two, (((1,), (1,)), ((), ())), preferred_element_type=jnp.float32)
                for h in range(2):
                    mat[2 * c + h, pl.ds(256 * r, 256), :] = SCALE * prod[:, 128 * h : 128 * h + 128] + penalty(h)
            return carry

        lax.fori_loop(0, TILES // 2, pair, 0)

    def lse(mat, col, out):
        def step(i, carry):
            tops, sums = [None] * WIDE, [None] * WIDE
            for r in range(PTS // 128):
                part = col[pl.ds(128 * r, 128), :]
                for h in range(WIDE):
                    v = mat[WIDE * i + h, pl.ds(128 * r, 128), :] + part
                    vs = [v[8 * n : 8 * n + 8, :] for n in range(16)]
                    top = tree(jnp.maximum, vs if r == 0 else vs + [tops[h]])
                    total = tree(jnp.add, [jnp.exp2(u - top) for u in vs])
                    sums[h] = total if r == 0 else sums[h] * jnp.exp2(tops[h] - top) + total
                    tops[h] = top
            for h in range(WIDE):
                top = jnp.max(tops[h], axis=0, keepdims=True)
                total = jnp.sum(sums[h] * jnp.exp2(tops[h] - top), axis=0, keepdims=True)
                out[pl.ds(WIDE * i + h, 1), :] = top + jnp.log2(total)
            return carry

        lax.fori_loop(0, TILES // WIDE, step, 0)

    def merge(ref, k):
        top = tree(jnp.maximum, [ref[k, i] for i in range(ref.shape[1])])
        total = tree(jnp.add, [jnp.exp2(ref[k, i] - top) for i in range(ref.shape[1])])
        return top + jnp.log2(total)

    for i, n in enumerate(LINE):
        got = tpeer(16 - 4 * n)
        done(xs.at[got], xsem.at[i, 1])
        for m in LINE:
            half = xs.at[got, pl.ds(0, 64)]
            push(half, half, xsem.at[6], {"tgt": tpeer(m)})
        got = tpeer(4 - n)
        done(xs.at[got], xsem.at[3 + i, 1])
        for m in LINE:
            half = xs.at[got, pl.ds(64, 64)]
            push(half, half, xsem.at[6], {"tgt": tpeer(4 * m)})
        piece = ys.at[pl.ds(speer(8 - 2 * n) * 2, 2)]
        done(piece, ysem.at[i, 1])
        push(piece, piece, ysem.at[4], {"src": speer(1)})
    done(ys.at[pl.ds(0, 2)], ysem.at[3, 1])
    done(ys.at[pl.ds(0, 6)], ysem.at[4, 1])
    done(tp.at[pl.ds(0, 14)], tpsem.at[1])
    done(xs.at[pl.ds(0, 9)], xsem.at[6, 1])
    done(sp.at[pl.ds(0, 15)], spsem.at[1])

    def rows_of(ref, r):
        return jnp.concatenate([ref[t, r : r + 1, :] for t in range(TILES)], axis=0)

    f, la, xh = rows_of(sp, 0), rows_of(sp, 1), rows_of(sp, 2)
    g, lb, yh = rows_of(tp, 0), rows_of(tp, 1), rows_of(tp, 2)
    la = la + sdead
    lb = lb + tdead
    spread(lb + SCALE * (g - yh), gb)
    spread(la + SCALE * (f - xh), fb)
    score(rmat, xs, ys, lambda h: pt[...], 256)

    def send_rows(k):
        rrecv[k, pl.ds(tgt, 1)] = rsend[k].reshape(1, 16, 128)
        for d in FAR_T:
            push(rsend.at[k], rrecv.at[k, tgt], rsem.at[k], {"tgt": tpeer(d)})

    def send_cols(k):
        crecv[k, pl.ds(src, 1)] = csend[k].reshape(1, 16, 128)
        for d in FAR_S:
            push(csend.at[k], crecv.at[k, src], csem.at[k], {"src": speer(d)})

    def take_rows(k, f):
        done(rrecv.at[k, pl.ds(0, 15)], rsem.at[k, 1])
        f = 0.5 * (f + (xh - merge(rrecv, k) * (1.0 / SCALE)))
        return f

    def take_cols(k, g):
        done(crecv.at[k, pl.ds(0, 7)], csem.at[k, 1])
        g = 0.5 * (g + (yh - merge(crecv, k) * (1.0 / SCALE)))
        return g

    lse(rmat, gb, rsend.at[0])
    send_rows(0)
    score(cmat, ys, xs, lambda h: jnp.concatenate([pn[h], pn[h]], axis=0), 256)
    ytr[128:144, :] = jnp.ones((16, PTS), jnp.bfloat16)
    for t in range(TILES):
        ytr[0:128, pl.ds(128 * t, 128)] = jnp.transpose(ys[t].astype(jnp.float32)).astype(jnp.bfloat16)
    lse(cmat, fb, csend.at[0])
    send_cols(0)
    for k in range(1, ITERS):
        if k % 2:
            f = take_rows(k - 1, f)
            spread(la + SCALE * (f - xh), fb)
            lse(cmat, fb, csend.at[k])
            send_cols(k)
            g = take_cols(k - 1, g)
            spread(lb + SCALE * (g - yh), gb)
            lse(rmat, gb, rsend.at[k])
            send_rows(k)
        else:
            g = take_cols(k - 1, g)
            spread(lb + SCALE * (g - yh), gb)
            lse(rmat, gb, rsend.at[k])
            send_rows(k)
            f = take_rows(k - 1, f)
            spread(la + SCALE * (f - xh), fb)
            lse(cmat, fb, csend.at[k])
            send_cols(k)
    g = take_cols(ITERS - 1, g)
    spread(lb + SCALE * (g - yh), gb)

    def project(i, carry):
        ds = [15 - 2 * i, 14 - 2 * i]
        cs = [lax.rem(tx + lax.div(d, 4), 4) * 4 + lax.rem(ty + lax.rem(d, 4), 4) for d in ds]
        tops = [[], []]
        for r in range(16):
            part = gb[pl.ds(128 * r, 128), :]
            for h in range(2):
                v = rmat[cs[h], pl.ds(128 * r, 128), :] + part
                vbuf[h, pl.ds(128 * r, 128), :] = v
                tops[h].append(fold(jnp.maximum, v))
        tops = [jnp.max(tree(jnp.maximum, t), axis=0, keepdims=True) for t in tops]
        for r in range(16):
            for h in range(2):
                w = jnp.exp2(vbuf[h, pl.ds(128 * r, 128), :] - tops[h])
                high = w.astype(jnp.bfloat16)
                whi[pl.ds(128 * r, 128), 128 * h : 128 * h + 128] = high
                wlo[pl.ds(128 * r, 128), 128 * h : 128 * h + 128] = (w - high.astype(jnp.float32)).astype(jnp.bfloat16)
        moved = jnp.dot(ytr[...], whi[...], preferred_element_type=jnp.float32) + jnp.dot(
            ytr[...], wlo[...], preferred_element_type=jnp.float32
        )
        r8 = iota((8, 128), 0)
        for h in range(2):
            msg[ds[h], 0:128, :] = moved[0:128, 128 * h : 128 * h + 128]
            total = moved[128:136, 128 * h : 128 * h + 128]
            msg[ds[h], 128:136, :] = jnp.where(r8 == 0, jnp.broadcast_to(tops[h], (8, 128)), total)
        push(msg.at[ds[0]], mrecv.at[ds[0]], msem, {"tgt": cs[0]})

        @pl.when(ds[1] > 0)
        def _():
            push(msg.at[ds[1]], mrecv.at[ds[1]], msem, {"tgt": cs[1]})

        return carry

    lax.fori_loop(0, 8, project, 0)
    f = take_rows(ITERS - 1, f)
    fb[0:16, :] = f
    f_out[...] = from_lanes(fb[pl.ds(tgt, 1), :], 16)
    gb[0:16, :] = g
    g_out[...] = from_lanes(gb[pl.ds(src * 2, 2), :], 32)
    mrecv[0] = msg[0]
    done(mrecv.at[pl.ds(1, 15)], msem.at[1])
    tops = [mrecv[d, 128:129, :] for d in range(16)]
    top = tree(jnp.maximum, tops)
    scales = [jnp.exp2(t - top) for t in tops]
    total = tree(jnp.add, [scales[d] * mrecv[d, 129:130, :] for d in range(16)])
    inv = 1.0 / total
    moved = scales[0] * mrecv[0, 0:128, :]
    for d in range(1, 16):
        moved = moved + scales[d] * mrecv[d, 0:128, :]
    img_out[...] = jnp.transpose(moved * inv)

    for i in range(6):
        done(xs.at[0], xsem.at[i, 0])
    done(xs.at[pl.ds(0, 9)], xsem.at[6, 0])
    for i in range(4):
        done(ys.at[pl.ds(0, 2)], ysem.at[i, 0])
    done(ys.at[pl.ds(0, 6)], ysem.at[4, 0])
    done(sp.at[pl.ds(0, 15)], spsem.at[0])
    done(tp.at[pl.ds(0, 14)], tpsem.at[0])
    for k in range(ITERS):
        done(rrecv.at[k, pl.ds(0, 15)], rsem.at[k, 0])
        done(crecv.at[k, pl.ds(0, 7)], csem.at[k, 0])
    done(mrecv.at[pl.ds(1, 15)], msem.at[0])


def on_device(src_points, tgt_points, src_mass, tgt_mass, src_potential, tgt_potential, src_counts, tgt_counts, keep):
    f32, bf16 = jnp.float32, jnp.bfloat16
    vmem = pl.BlockSpec(memory_space=pltpu.VMEM)
    smem = pl.BlockSpec(memory_space=pltpu.SMEM)
    dma = pltpu.SemaphoreType.DMA
    images, f, g = pl.pallas_call(
        kernel,
        out_shape=(
            jax.ShapeDtypeStruct((128, 128), f32),
            jax.ShapeDtypeStruct((8, 16), f32),
            jax.ShapeDtypeStruct((8, 32), f32),
        ),
        in_specs=[smem] * 3 + [vmem] * 6,
        out_specs=(vmem, vmem, vmem),
        scratch_shapes=[
            pltpu.VMEM((16, 128, 128), bf16),
            pltpu.VMEM((16, 128, 128), bf16),
            pltpu.VMEM((16, 8, 128), f32),
            pltpu.VMEM((16, 8, 128), f32),
            pltpu.VMEM((144, PTS), bf16),
            pltpu.VMEM((16, PTS, 128), f32),
            pltpu.VMEM((16, PTS, 128), f32),
            pltpu.VMEM((2, PTS, 128), f32),
            pltpu.VMEM((PTS, 128), f32),
            pltpu.VMEM((PTS, 128), f32),
            pltpu.VMEM((2, 128, 128), f32),
            pltpu.VMEM((256, 128), f32),
            pltpu.VMEM((PTS, 256), bf16),
            pltpu.VMEM((PTS, 256), bf16),
            pltpu.VMEM((8, 128), f32),
            pltpu.VMEM((2, 8, 128), f32),
            pltpu.VMEM((ITERS, 16, 128), f32),
            pltpu.VMEM((ITERS, 16, 16, 128), f32),
            pltpu.VMEM((ITERS, 16, 128), f32),
            pltpu.VMEM((ITERS, 8, 16, 128), f32),
            pltpu.VMEM((16, 136, 128), f32),
            pltpu.VMEM((16, 136, 128), f32),
            dma((7, 2)),
            dma((2,)),
            dma((5, 2)),
            dma((2,)),
            dma((ITERS, 2)),
            dma((ITERS, 2)),
            dma((2,)),
        ],
        compiler_params=pltpu.CompilerParams(
            collective_id=0, has_side_effects=True, vmem_limit_bytes=60 * 1024 * 1024
        ),
        name="sinkhorn",
    )(
        src_counts,
        tgt_counts,
        keep,
        src_points.reshape(128, 128),
        tgt_points.reshape(2, 128, 128),
        src_mass,
        tgt_mass,
        src_potential,
        tgt_potential,
    )
    return images.reshape(8, 16, 128), f, g


def solution(mesh):
    return jax.shard_map(
        on_device,
        mesh=mesh,
        in_specs=(
            P("src", "tgt", None),
            P("tgt", "src", None),
            P("src", "tgt"),
            P("tgt", "src"),
            P("src", "tgt"),
            P("tgt", "src"),
            P("src"),
            P("tgt"),
            P("src", "tgt"),
        ),
        out_specs=(P("src", "tgt", None), P("src", "tgt"), P("tgt", "src")),
        check_vma=False,
    )
```

```python
import math

import jax
import jax.numpy as jnp
from jax import lax
from jax.experimental import pallas as pl
from jax.experimental.pallas import tpu as pltpu
from jax.sharding import PartitionSpec as P

ITERS = 4
EPSILON = 0.1
NEG = -1e30
SCALE = math.log2(math.e) / EPSILON
MESH = pl.DeviceIdType.MESH

NT, NS = 16, 8
PTS = 2048
TILES = 16
WIDE = 4
FAR_T = sorted(range(1, NT), key=lambda d: -(min(d // 4, 4 - d // 4) + min(d % 4, 4 - d % 4)))
LINE = (1, 3, 2)
FAR_S = sorted(range(1, NS), key=lambda d: -(2 * min(d // 2, 4 - d // 2) + d % 2))


def iota(shape, dim):
    return lax.broadcasted_iota(jnp.int32, shape, dim)


def tree(op, parts):
    parts = list(parts)
    while len(parts) > 1:
        parts = [op(parts[i], parts[i + 1]) if i + 1 < len(parts) else parts[i] for i in range(0, len(parts), 2)]
    return parts[0]


def fold(op, block):
    return tree(op, [block[8 * i : 8 * i + 8, :] for i in range(block.shape[0] // 8)])


def to_lanes(block):
    n = block.shape[1]
    put = (iota((n, 8 * n), 1) % n == iota((n, 8 * n), 0)).astype(jnp.bfloat16)
    wide = jnp.dot(block, put, preferred_element_type=jnp.float32)
    own = iota((8, 8 * n), 1) // n == iota((8, 8 * n), 0)
    return jnp.sum(jnp.where(own, wide, 0.0), axis=0, keepdims=True)


def thirds(wide):
    high = wide.astype(jnp.bfloat16)
    rest = wide - high.astype(jnp.float32)
    mid = rest.astype(jnp.bfloat16)
    return high, mid, (rest - mid.astype(jnp.float32)).astype(jnp.bfloat16)


def from_lanes(rows, n):
    per = 128 // n
    home, lane = iota((8, 128), 0), iota((8, 128), 1)
    wide = jnp.zeros((8, 128), jnp.float32)
    for h in range(rows.shape[0]):
        wide = jnp.where(home == h * per + lane // n, jnp.broadcast_to(rows[h : h + 1, :], (8, 128)), wide)
    put = (iota((128, n), 0) % n == iota((128, n), 1)).astype(jnp.bfloat16)
    parts = [jnp.dot(part, put, preferred_element_type=jnp.float32) for part in thirds(wide)]
    return parts[0] + parts[1] + parts[2]


def half_norm(points):
    wide = points.astype(jnp.float32)
    square = wide * wide
    high = square.astype(jnp.bfloat16)
    low = (square - high.astype(jnp.float32)).astype(jnp.bfloat16)
    ones = jnp.ones((8, 128), jnp.bfloat16)
    dims = (((1,), (1,)), ((), ()))
    total = lax.dot_general(ones, high, dims, preferred_element_type=jnp.float32) + lax.dot_general(
        ones, low, dims, preferred_element_type=jnp.float32
    )
    return 0.5 * total[0:1, :]


def kernel(
    scnt, tcnt, keep, x_in, y_in, a_in, b_in, f_in, g_in, img_out, f_out, g_out,
    xs, ys, sp, tp, ytr, cmat, rmat, vbuf, fb, gb, sel, pt, whi, wlo, fl, gl,
    rsend, rrecv, csend, crecv, msg, mrecv, stat, srecv,
    xsem, spsem, ysem, tpsem, rsem, csem, msem, ssem, kept,
):
    src = lax.axis_index("src")
    tgt = lax.axis_index("tgt")
    sz, sc = lax.div(src, 2), lax.rem(src, 2)
    tx, ty = lax.div(tgt, 4), lax.rem(tgt, 4)

    def tpeer(d):
        return lax.rem(tx + d // 4, 4) * 4 + lax.rem(ty + d % 4, 4)

    def speer(d):
        return lax.rem(sz + d // 2, 4) * 2 + lax.rem(sc + d % 2, 2)

    barrier = pltpu.get_barrier_semaphore()
    for n in LINE:
        pl.semaphore_signal(barrier, inc=1, device_id={"tgt": tpeer(4 * n)}, device_id_type=MESH)
        pl.semaphore_signal(barrier, inc=1, device_id={"tgt": tpeer(n)}, device_id_type=MESH)
        pl.semaphore_signal(barrier, inc=1, device_id={"src": speer(2 * n)}, device_id_type=MESH)
    pl.semaphore_signal(barrier, inc=1, device_id={"src": speer(1)}, device_id_type=MESH)

    def push(source, dest, sem, device):
        pltpu.make_async_remote_copy(
            src_ref=source, dst_ref=dest, send_sem=sem.at[0], recv_sem=sem.at[1], device_id=device, device_id_type=MESH
        ).start()

    def done(ref, sem):
        pltpu.make_async_copy(ref, ref, sem).wait()

    lane = iota((1, 128), 1)
    xs[pl.ds(tgt, 1)] = x_in[...].reshape(1, 128, 128)
    ys[pl.ds(src * 2, 2)] = y_in[...].reshape(2, 128, 128)
    fl[...] = jnp.zeros((8, 128), jnp.float32)
    gl[...] = jnp.zeros((2, 8, 128), jnp.float32)
    fl[0:1, :] = to_lanes(f_in[...])
    fl[1:2, :] = jnp.log2(to_lanes(a_in[...]))
    fl[2:3, :] = half_norm(x_in[...])
    tgt_rows = (to_lanes(g_in[...]), jnp.log2(to_lanes(b_in[...])), half_norm(y_in[...].reshape(256, 128)))
    for r, row in enumerate(tgt_rows):
        for h in range(2):
            gl[h, r : r + 1, :] = row[:, 128 * h : 128 * h + 128]
    sp[pl.ds(tgt, 1)] = fl[...].reshape(1, 8, 128)
    tp[pl.ds(src * 2, 2)] = gl[...]

    pl.semaphore_wait(barrier, 10)
    mine_y = pl.ds(src * 2, 2)
    for i, n in enumerate(LINE):
        push(fl, sp.at[tgt], spsem.at[i], {"tgt": tpeer(4 * n)})
        push(fl, sp.at[tgt], spsem.at[3], {"tgt": tpeer(n)})
        push(gl, tp.at[mine_y], tpsem.at[i], {"src": speer(2 * n)})
        push(x_in, xs.at[tgt], xsem.at[i], {"tgt": tpeer(4 * n)})
        push(x_in, xs.at[tgt], xsem.at[3 + i], {"tgt": tpeer(n)})
        push(y_in, ys.at[mine_y], ysem.at[i], {"src": speer(2 * n)})
    push(gl, tp.at[mine_y], tpsem.at[3], {"src": speer(1)})
    push(y_in, ys.at[mine_y], ysem.at[3], {"src": speer(1)})

    for q in range(8):
        row = jnp.zeros((1, 128), jnp.float32)
        for p in range(8):
            pen = jnp.where(keep[p, q] > 0, 0.0, NEG)
            row = jnp.where(lane // 16 == p, pen, row)
        pt[pl.ds(32 * q, 32), :] = jnp.broadcast_to(row, (32, 128))
    r16, l16 = iota((16, 128), 0), iota((16, 128), 1)
    sdead = jnp.zeros((16, 128), jnp.float32)
    tdead = jnp.zeros((16, 128), jnp.float32)
    for p in range(8):
        sdead = jnp.where((l16 // 16 == p) & (r16 * 16 + l16 % 16 >= scnt[p]), NEG, sdead)
        tdead = jnp.where(((r16 % 2) * 4 + l16 // 32 == p) & ((r16 // 2) * 32 + l16 % 32 >= tcnt[p]), NEG, tdead)
    sel[...] = (iota((48, PTS), 0) % 16 == iota((48, PTS), 1) // 128).astype(jnp.bfloat16)

    def spread(rows, dest, halves=(0, 1)):
        parts = jnp.concatenate(thirds(rows), axis=0)
        for half in halves:
            wide = lax.dot_general(
                parts, sel[:, 1024 * half : 1024 * half + 1024], (((0,), (0,)), ((), ())), preferred_element_type=jnp.float32
            )
            for t in range(8):
                dest[pl.ds(1024 * half + 128 * t, 128), :] = wide[:, 128 * t : 128 * t + 128]

    def running(part, block, top, total):
        vs = [block[8 * n : 8 * n + 8, :] + part[8 * n : 8 * n + 8, :] for n in range(16)]
        new = tree(jnp.maximum, vs if top is None else vs + [top])
        more = tree(jnp.add, [jnp.exp2(u - new) for u in vs])
        return new, more if top is None else total * jnp.exp2(top - new) + more

    def close(out, c, top8, total8):
        top = jnp.max(top8, axis=0, keepdims=True)
        total = jnp.sum(total8 * jnp.exp2(top8 - top), axis=0, keepdims=True)
        out[pl.ds(c, 1), :] = top + jnp.log2(total)

    def first(i, carry):
        k = i // 2
        dx = k + (k // 2) * (1 - 2 * (k % 2))

        @pl.when((i % 2 == 0) & (i > 0))
        def _():
            done(xs.at[pl.ds(0, 3)], xsem.at[5 + k, 1])

        c = lax.rem(tx + 4 - dx, 4) * 4 + 2 * (i % 2)
        two = jnp.transpose(xs[pl.ds(c, 2)].reshape(256, 128).astype(jnp.float32)).astype(jnp.bfloat16)
        state = [(None, None)] * 2
        for r in range(8):
            prod = jnp.dot(ys[2 * r : 2 * r + 2].reshape(256, 128), two, preferred_element_type=jnp.float32)
            for v in range(2):
                j = 2 * r + v
                part = gb[pl.ds(128 * j, 128), :]
                for h in range(2):
                    block = SCALE * prod[128 * v : 128 * v + 128, 128 * h : 128 * h + 128] + pt[128 * v : 128 * v + 128, :]
                    rmat[c + h, pl.ds(128 * j, 128), :] = block
                    cmat[j, pl.ds(128 * (c + h), 128), :] = jnp.transpose(block)
                    state[h] = running(part, block, *state[h])
        for h in range(2):
            close(rsend.at[0], c + h, *state[h])
        return carry

    def lse(mat, col, out, lo, hi):
        def step(i, carry):
            state = [(None, None)] * WIDE
            for r in range(PTS // 128):
                part = col[pl.ds(128 * r, 128), :]
                for h in range(WIDE):
                    state[h] = running(part, mat[WIDE * i + h, pl.ds(128 * r, 128), :], *state[h])
            for h in range(WIDE):
                close(out, WIDE * i + h, *state[h])
            return carry

        lax.fori_loop(lo // WIDE, hi // WIDE, step, 0)

    def lse_part(mat, col, out, half):
        def step(i, carry):
            tiles = [WIDE * i + h for h in range(WIDE)]
            state = [(kept[c, 0], kept[c, 1]) if half else (None, None) for c in tiles]
            for r in range(8 * half, 8 * half + 8):
                part = col[pl.ds(128 * r, 128), :]
                for h in range(WIDE):
                    state[h] = running(part, mat[tiles[h], pl.ds(128 * r, 128), :], *state[h])
            for h in range(WIDE):
                if half:
                    close(out, tiles[h], *state[h])
                else:
                    kept[tiles[h], 0] = state[h][0]
                    kept[tiles[h], 1] = state[h][1]
            return carry

        lax.fori_loop(0, TILES // WIDE, step, 0)

    def merge(parts):
        top = tree(jnp.maximum, parts)
        return top + jnp.log2(tree(jnp.add, [jnp.exp2(part - top) for part in parts]))

    for i, n in enumerate(LINE):
        got = tpeer(16 - 4 * n)
        done(sp.at[got], spsem.at[i, 1])
        for m in LINE:
            push(sp.at[got], sp.at[got], spsem.at[3], {"tgt": tpeer(m)})
        piece = tp.at[pl.ds(speer(8 - 2 * n) * 2, 2)]
        done(piece, tpsem.at[i, 1])
        push(piece, piece, tpsem.at[3], {"src": speer(1)})
        done(xs.at[got], xsem.at[i, 1])
        for m in LINE:
            half = xs.at[got, pl.ds(0, 64)]
            push(half, half, xsem.at[6 + i], {"tgt": tpeer(m)})
        got = tpeer(4 - n)
        done(xs.at[got], xsem.at[3 + i, 1])
        for m in LINE:
            half = xs.at[got, pl.ds(64, 64)]
            push(half, half, xsem.at[6 + LINE.index(m)], {"tgt": tpeer(4 * m)})
        piece = ys.at[pl.ds(speer(8 - 2 * n) * 2, 2)]
        done(piece, ysem.at[i, 1])
        push(piece, piece, ysem.at[4], {"src": speer(1)})
    def rows_of(ref, r):
        return jnp.concatenate([ref[t, r : r + 1, :] for t in range(TILES)], axis=0)

    done(tp.at[pl.ds(0, 8)], tpsem.at[3, 1])
    g, lb, yh = rows_of(tp, 0), rows_of(tp, 1), rows_of(tp, 2)
    lb = lb + tdead
    spread(lb + SCALE * (g - yh), gb)
    done(ys.at[pl.ds(0, 2)], ysem.at[3, 1])
    done(ys.at[pl.ds(0, 6)], ysem.at[4, 1])

    def send_rows(k, lo, hi):
        piece = pl.ds(lo, hi - lo)
        rrecv[k, pl.ds(tgt, 1), piece] = rsend[k, piece].reshape(1, hi - lo, 128)
        for d in FAR_T:
            push(rsend.at[k, piece], rrecv.at[k, tgt, piece], rsem.at[k, lo // 8], {"tgt": tpeer(d)})

    def send_cols(k):
        crecv[k, pl.ds(src, 1)] = csend[k].reshape(1, 16, 128)
        for d in FAR_S:
            push(csend.at[k], crecv.at[k, src], csem.at[k], {"src": speer(d)})

    def take_rows(k, f, half):
        piece = pl.ds(8 * half, 8)
        done(rrecv.at[k, pl.ds(0, 15), piece], rsem.at[k, half, 1])
        whole = merge([rrecv[k, i, piece] for i in range(NT)])
        return 0.5 * (f + (xh[8 * half : 8 * half + 8] - whole * (1.0 / SCALE)))

    def take_cols(k, g):
        done(crecv.at[k, pl.ds(0, 7)], csem.at[k, 1])
        return 0.5 * (g + (yh - merge([crecv[k, i] for i in range(NS)]) * (1.0 / SCALE)))

    lax.fori_loop(0, TILES // 2, first, 0)
    send_rows(0, 0, 8)
    send_rows(0, 8, 16)
    done(sp.at[pl.ds(0, 12)], spsem.at[3, 1])
    f, la, xh = rows_of(sp, 0), rows_of(sp, 1), rows_of(sp, 2)
    la = la + sdead
    spread(la + SCALE * (f - xh), fb)
    f = [f[0:8], f[8:16]]
    lse(cmat, fb, csend.at[0], 0, 16)
    send_cols(0)
    ytr[128:144, :] = jnp.ones((16, PTS), jnp.bfloat16)
    for t in range(TILES):
        ytr[0:128, pl.ds(128 * t, 128)] = jnp.transpose(ys[t].astype(jnp.float32)).astype(jnp.bfloat16)

    def row_half(k, g):
        g = take_cols(k - 1, g)
        spread(lb + SCALE * (g - yh), gb)
        for lo in (0, 8):
            lse(rmat, gb, rsend.at[k], lo, lo + 8)
            send_rows(k, lo, lo + 8)
        return g

    def col_half(k, f):
        f = list(f)
        for half in range(2):
            f[half] = take_rows(k - 1, f[half], half)
            at = slice(8 * half, 8 * half + 8)
            rows = la[at] + SCALE * (f[half] - xh[at])
            zero = jnp.zeros((8, 128), jnp.float32)
            spread(jnp.concatenate([zero, rows] if half else [rows, zero], axis=0), fb, (half,))
            lse_part(cmat, fb, csend.at[k], half)
        send_cols(k)
        return f

    for k in range(1, ITERS):
        if k % 2:
            f = col_half(k, f)
            g = row_half(k, g)
        else:
            g = row_half(k, g)
            f = col_half(k, f)
    g = take_cols(ITERS - 1, g)
    spread(lb + SCALE * (g - yh), gb)

    def project(i, carry):
        ds = [15 - 2 * i, 14 - 2 * i]
        cs = [lax.rem(tx + lax.div(d, 4), 4) * 4 + lax.rem(ty + lax.rem(d, 4), 4) for d in ds]
        tops = [[], []]
        for r in range(16):
            part = gb[pl.ds(128 * r, 128), :]
            for h in range(2):
                v = rmat[cs[h], pl.ds(128 * r, 128), :] + part
                vbuf[h, pl.ds(128 * r, 128), :] = v
                tops[h].append(fold(jnp.maximum, v))
        tops = [jnp.max(tree(jnp.maximum, t), axis=0, keepdims=True) for t in tops]
        for r in range(16):
            for h in range(2):
                w = jnp.exp2(vbuf[h, pl.ds(128 * r, 128), :] - tops[h])
                high = w.astype(jnp.bfloat16)
                whi[pl.ds(128 * r, 128), 128 * h : 128 * h + 128] = high
                wlo[pl.ds(128 * r, 128), 128 * h : 128 * h + 128] = (w - high.astype(jnp.float32)).astype(jnp.bfloat16)
        moved = jnp.dot(ytr[...], whi[...], preferred_element_type=jnp.float32) + jnp.dot(
            ytr[...], wlo[...], preferred_element_type=jnp.float32
        )
        r8 = iota((8, 128), 0)
        for h in range(2):
            block = moved[0:128, 128 * h : 128 * h + 128]
            most = jnp.max(fold(jnp.maximum, jnp.abs(block)), axis=0, keepdims=True)
            most = jnp.maximum(most, 1e-30)
            msg[ds[h]] = jnp.round(block * (32767.0 / most)).astype(jnp.int32).astype(jnp.int16)
            rows = (tops[h], moved[128:129, 128 * h : 128 * h + 128], most * (1.0 / 32767.0))
            stat[ds[h]] = tree(jnp.add, [jnp.where(r8 == n, jnp.broadcast_to(row, (8, 128)), 0.0) for n, row in enumerate(rows)])
        push(stat.at[ds[0]], srecv.at[ds[0]], ssem, {"tgt": cs[0]})
        push(msg.at[ds[0]], mrecv.at[ds[0]], msem, {"tgt": cs[0]})

        @pl.when(ds[1] > 0)
        def _():
            push(stat.at[ds[1]], srecv.at[ds[1]], ssem, {"tgt": cs[1]})
            push(msg.at[ds[1]], mrecv.at[ds[1]], msem, {"tgt": cs[1]})

        return carry

    lax.fori_loop(0, 8, project, 0)
    for half in range(2):
        fb[8 * half : 8 * half + 8, :] = take_rows(ITERS - 1, f[half], half)
    f_out[...] = from_lanes(fb[pl.ds(tgt, 1), :], 16)
    gb[0:16, :] = g
    g_out[...] = from_lanes(gb[pl.ds(src * 2, 2), :], 32)
    mrecv[0] = msg[0]
    srecv[0] = stat[0]
    done(srecv.at[pl.ds(1, 15)], ssem.at[1])
    tops = [srecv[d, 0:1, :] for d in range(16)]
    top = tree(jnp.maximum, tops)
    scales = [jnp.exp2(t - top) for t in tops]
    inv = 1.0 / tree(jnp.add, [scales[d] * srecv[d, 1:2, :] for d in range(16)])
    scales = [scales[d] * srecv[d, 2:3, :] * inv for d in range(16)]
    done(mrecv.at[pl.ds(1, 15)], msem.at[1])
    moved = tree(jnp.add, [scales[d] * mrecv[d].astype(jnp.int32).astype(jnp.float32) for d in range(16)])
    img_out[...] = jnp.transpose(moved)

    for i in range(6):
        done(xs.at[0], xsem.at[i, 0])
    for i in range(3):
        done(xs.at[pl.ds(0, 3)], xsem.at[6 + i, 0])
    for i in range(4):
        done(ys.at[pl.ds(0, 2)], ysem.at[i, 0])
    done(ys.at[pl.ds(0, 6)], ysem.at[4, 0])
    for i in range(3):
        done(sp.at[0], spsem.at[i, 0])
        done(tp.at[pl.ds(0, 2)], tpsem.at[i, 0])
    done(sp.at[pl.ds(0, 12)], spsem.at[3, 0])
    done(tp.at[pl.ds(0, 8)], tpsem.at[3, 0])
    for k in range(ITERS):
        for half in range(2):
            done(rrecv.at[k, pl.ds(0, 15), pl.ds(8 * half, 8)], rsem.at[k, half, 0])
        done(crecv.at[k, pl.ds(0, 7)], csem.at[k, 0])
    done(mrecv.at[pl.ds(1, 15)], msem.at[0])
    done(srecv.at[pl.ds(1, 15)], ssem.at[0])


def on_device(src_points, tgt_points, src_mass, tgt_mass, src_potential, tgt_potential, src_counts, tgt_counts, keep):
    f32, bf16 = jnp.float32, jnp.bfloat16
    vmem = pl.BlockSpec(memory_space=pltpu.VMEM)
    smem = pl.BlockSpec(memory_space=pltpu.SMEM)
    dma = pltpu.SemaphoreType.DMA
    images, f, g = pl.pallas_call(
        kernel,
        out_shape=(
            jax.ShapeDtypeStruct((128, 128), f32),
            jax.ShapeDtypeStruct((8, 16), f32),
            jax.ShapeDtypeStruct((8, 32), f32),
        ),
        in_specs=[smem] * 3 + [vmem] * 6,
        out_specs=(vmem, vmem, vmem),
        scratch_shapes=[
            pltpu.VMEM((16, 128, 128), bf16),
            pltpu.VMEM((16, 128, 128), bf16),
            pltpu.VMEM((16, 8, 128), f32),
            pltpu.VMEM((16, 8, 128), f32),
            pltpu.VMEM((144, PTS), bf16),
            pltpu.VMEM((16, PTS, 128), f32),
            pltpu.VMEM((16, PTS, 128), f32),
            pltpu.VMEM((2, PTS, 128), f32),
            pltpu.VMEM((PTS, 128), f32),
            pltpu.VMEM((PTS, 128), f32),
            pltpu.VMEM((48, PTS), bf16),
            pltpu.VMEM((256, 128), f32),
            pltpu.VMEM((PTS, 256), bf16),
            pltpu.VMEM((PTS, 256), bf16),
            pltpu.VMEM((8, 128), f32),
            pltpu.VMEM((2, 8, 128), f32),
            pltpu.VMEM((ITERS, 16, 128), f32),
            pltpu.VMEM((ITERS, 16, 16, 128), f32),
            pltpu.VMEM((ITERS, 16, 128), f32),
            pltpu.VMEM((ITERS, 8, 16, 128), f32),
            pltpu.VMEM((16, 128, 128), jnp.int16),
            pltpu.VMEM((16, 128, 128), jnp.int16),
            pltpu.VMEM((16, 8, 128), f32),
            pltpu.VMEM((16, 8, 128), f32),
            dma((9, 2)),
            dma((4, 2)),
            dma((5, 2)),
            dma((4, 2)),
            dma((ITERS, 2, 2)),
            dma((ITERS, 2)),
            dma((2,)),
            dma((2,)),
            pltpu.VMEM((TILES, 2, 8, 128), f32),
        ],
        compiler_params=pltpu.CompilerParams(
            collective_id=0, has_side_effects=True, vmem_limit_bytes=60 * 1024 * 1024
        ),
        name="sinkhorn",
    )(
        src_counts,
        tgt_counts,
        keep,
        src_points.reshape(128, 128),
        tgt_points.reshape(2, 128, 128),
        src_mass,
        tgt_mass,
        src_potential,
        tgt_potential,
    )
    return images.reshape(8, 16, 128), f, g


def solution(mesh):
    return jax.shard_map(
        on_device,
        mesh=mesh,
        in_specs=(
            P("src", "tgt", None),
            P("tgt", "src", None),
            P("src", "tgt"),
            P("tgt", "src"),
            P("src", "tgt"),
            P("tgt", "src"),
            P("src"),
            P("tgt"),
            P("src", "tgt"),
        ),
        out_specs=(P("src", "tgt", None), P("src", "tgt"), P("tgt", "src")),
        check_vma=False,
    )
```

```python
import math

import jax
import jax.numpy as jnp
from jax import lax
from jax.experimental import pallas as pl
from jax.experimental.pallas import tpu as pltpu
from jax.sharding import PartitionSpec as P

ITERS = 4
EPSILON = 0.1
NEG = -1e30
SCALE = math.log2(math.e) / EPSILON
MESH = pl.DeviceIdType.MESH

NT, NS = 16, 8
PTS = 2048
TILES = 16
WIDE = 4
FAR_T = sorted(range(1, NT), key=lambda d: -(min(d // 4, 4 - d // 4) + min(d % 4, 4 - d % 4)))
LINE = (1, 3, 2)
ORDER = FAR_T + [0]
FAR_S = sorted(range(1, NS), key=lambda d: -(2 * min(d // 2, 4 - d // 2) + d % 2))


def iota(shape, dim):
    return lax.broadcasted_iota(jnp.int32, shape, dim)


def pick(i, values):
    return sum(jnp.where(i == n, v, 0) for n, v in enumerate(values))


def tree(op, parts):
    parts = list(parts)
    while len(parts) > 1:
        parts = [op(parts[i], parts[i + 1]) if i + 1 < len(parts) else parts[i] for i in range(0, len(parts), 2)]
    return parts[0]


def fold(op, block):
    return tree(op, [block[8 * i : 8 * i + 8, :] for i in range(block.shape[0] // 8)])


def to_lanes(block):
    n = block.shape[1]
    put = (iota((n, 8 * n), 1) % n == iota((n, 8 * n), 0)).astype(jnp.bfloat16)
    wide = jnp.dot(block, put, preferred_element_type=jnp.float32)
    own = iota((8, 8 * n), 1) // n == iota((8, 8 * n), 0)
    return jnp.sum(jnp.where(own, wide, 0.0), axis=0, keepdims=True)


def thirds(wide):
    high = wide.astype(jnp.bfloat16)
    rest = wide - high.astype(jnp.float32)
    mid = rest.astype(jnp.bfloat16)
    return high, mid, (rest - mid.astype(jnp.float32)).astype(jnp.bfloat16)


def from_lanes(rows, n):
    per = 128 // n
    home, lane = iota((8, 128), 0), iota((8, 128), 1)
    wide = jnp.zeros((8, 128), jnp.float32)
    for h in range(rows.shape[0]):
        wide = jnp.where(home == h * per + lane // n, jnp.broadcast_to(rows[h : h + 1, :], (8, 128)), wide)
    put = (iota((128, n), 0) % n == iota((128, n), 1)).astype(jnp.bfloat16)
    parts = [jnp.dot(part, put, preferred_element_type=jnp.float32) for part in thirds(wide)]
    return parts[0] + parts[1] + parts[2]


def half_norm(points):
    wide = points.astype(jnp.float32)
    square = wide * wide
    high = square.astype(jnp.bfloat16)
    low = (square - high.astype(jnp.float32)).astype(jnp.bfloat16)
    ones = jnp.ones((8, 128), jnp.bfloat16)
    dims = (((1,), (1,)), ((), ()))
    total = lax.dot_general(ones, high, dims, preferred_element_type=jnp.float32) + lax.dot_general(
        ones, low, dims, preferred_element_type=jnp.float32
    )
    return 0.5 * total[0:1, :]


def kernel(
    scnt, tcnt, keep, x_in, y_in, a_in, b_in, f_in, g_in, img_out, f_out, g_out,
    xs, ys, sp, tp, ytr, cmat, rmat, vbuf, fb, gb, sel, pt, whi, wlo, fl, gl,
    rsend, rrecv, csend, crecv, msg, mrecv, stat, srecv,
    xsem, spsem, ysem, tpsem, rsem, csem, msem, ssem, kept,
):
    src = lax.axis_index("src")
    tgt = lax.axis_index("tgt")
    sz, sc = lax.div(src, 2), lax.rem(src, 2)
    tx, ty = lax.div(tgt, 4), lax.rem(tgt, 4)

    def tpeer(d):
        return lax.rem(tx + d // 4, 4) * 4 + lax.rem(ty + d % 4, 4)

    def speer(d):
        return lax.rem(sz + d // 2, 4) * 2 + lax.rem(sc + d % 2, 2)

    barrier = pltpu.get_barrier_semaphore()
    for n in LINE:
        pl.semaphore_signal(barrier, inc=1, device_id={"tgt": tpeer(4 * n)}, device_id_type=MESH)
        pl.semaphore_signal(barrier, inc=1, device_id={"tgt": tpeer(n)}, device_id_type=MESH)
        pl.semaphore_signal(barrier, inc=1, device_id={"src": speer(2 * n)}, device_id_type=MESH)
    pl.semaphore_signal(barrier, inc=1, device_id={"src": speer(1)}, device_id_type=MESH)

    def push(source, dest, sem, device):
        pltpu.make_async_remote_copy(
            src_ref=source, dst_ref=dest, send_sem=sem.at[0], recv_sem=sem.at[1], device_id=device, device_id_type=MESH
        ).start()

    def done(ref, sem):
        pltpu.make_async_copy(ref, ref, sem).wait()

    lane = iota((1, 128), 1)
    xs[pl.ds(tgt, 1)] = x_in[...].reshape(1, 128, 128)
    ys[pl.ds(src * 2, 2)] = y_in[...].reshape(2, 128, 128)
    fl[...] = jnp.zeros((8, 128), jnp.float32)
    gl[...] = jnp.zeros((2, 8, 128), jnp.float32)
    fl[0:1, :] = to_lanes(f_in[...])
    fl[1:2, :] = jnp.log2(to_lanes(a_in[...]))
    fl[2:3, :] = half_norm(x_in[...])
    tgt_rows = (to_lanes(g_in[...]), jnp.log2(to_lanes(b_in[...])), half_norm(y_in[...].reshape(256, 128)))
    for r, row in enumerate(tgt_rows):
        for h in range(2):
            gl[h, r : r + 1, :] = row[:, 128 * h : 128 * h + 128]
    sp[pl.ds(tgt, 1)] = fl[...].reshape(1, 8, 128)
    tp[pl.ds(src * 2, 2)] = gl[...]

    pl.semaphore_wait(barrier, 10)
    mine_y = pl.ds(src * 2, 2)
    for i, n in enumerate(LINE):
        push(fl, sp.at[tgt], spsem.at[i], {"tgt": tpeer(4 * n)})
        push(fl, sp.at[tgt], spsem.at[3], {"tgt": tpeer(n)})
        push(gl, tp.at[mine_y], tpsem.at[i], {"src": speer(2 * n)})
        push(x_in, xs.at[tgt], xsem.at[i], {"tgt": tpeer(4 * n)})
        push(x_in, xs.at[tgt], xsem.at[3 + i], {"tgt": tpeer(n)})
        push(y_in, ys.at[mine_y], ysem.at[i], {"src": speer(2 * n)})
    push(gl, tp.at[mine_y], tpsem.at[3], {"src": speer(1)})
    push(y_in, ys.at[mine_y], ysem.at[3], {"src": speer(1)})

    for q in range(8):
        row = jnp.zeros((1, 128), jnp.float32)
        for p in range(8):
            pen = jnp.where(keep[p, q] > 0, 0.0, NEG)
            row = jnp.where(lane // 16 == p, pen, row)
        pt[pl.ds(32 * q, 32), :] = jnp.broadcast_to(row, (32, 128))
    r16, l16 = iota((16, 128), 0), iota((16, 128), 1)
    sdead = jnp.zeros((16, 128), jnp.float32)
    tdead = jnp.zeros((16, 128), jnp.float32)
    for p in range(8):
        sdead = jnp.where((l16 // 16 == p) & (r16 * 16 + l16 % 16 >= scnt[p]), NEG, sdead)
        tdead = jnp.where(((r16 % 2) * 4 + l16 // 32 == p) & ((r16 // 2) * 32 + l16 % 32 >= tcnt[p]), NEG, tdead)
    sel[...] = (iota((48, PTS), 0) % 16 == iota((48, PTS), 1) // 128).astype(jnp.bfloat16)

    def spread(rows, dest, halves=(0, 1)):
        parts = jnp.concatenate(thirds(rows), axis=0)
        for half in halves:
            wide = lax.dot_general(
                parts, sel[:, 1024 * half : 1024 * half + 1024], (((0,), (0,)), ((), ())), preferred_element_type=jnp.float32
            )
            for t in range(8):
                dest[pl.ds(1024 * half + 128 * t, 128), :] = wide[:, 128 * t : 128 * t + 128]

    def running(part, block, top, total):
        vs = [block[8 * n : 8 * n + 8, :] + part[8 * n : 8 * n + 8, :] for n in range(16)]
        new = tree(jnp.maximum, vs if top is None else vs + [top])
        more = tree(jnp.add, [jnp.exp2(u - new) for u in vs])
        return new, more if top is None else total * jnp.exp2(top - new) + more

    def close(out, c, top8, total8):
        top = jnp.max(top8, axis=0, keepdims=True)
        total = jnp.sum(total8 * jnp.exp2(top8 - top), axis=0, keepdims=True)
        out[pl.ds(c, 1), :] = top + jnp.log2(total)

    def first(i, carry):
        k = i // 2
        dx = k + (k // 2) * (1 - 2 * (k % 2))

        @pl.when((i % 2 == 0) & (i > 0))
        def _():
            done(xs.at[pl.ds(0, 3)], xsem.at[5 + k, 1])

        c = lax.rem(tx + 4 - dx, 4) * 4 + 2 * (i % 2)
        two = jnp.transpose(xs[pl.ds(c, 2)].reshape(256, 128).astype(jnp.float32)).astype(jnp.bfloat16)
        state = [(None, None)] * 2
        for r in range(8):
            prod = jnp.dot(ys[2 * r : 2 * r + 2].reshape(256, 128), two, preferred_element_type=jnp.float32)
            for v in range(2):
                j = 2 * r + v
                part = gb[pl.ds(128 * j, 128), :]
                for h in range(2):
                    block = SCALE * prod[128 * v : 128 * v + 128, 128 * h : 128 * h + 128] + pt[128 * v : 128 * v + 128, :]
                    rmat[c + h, pl.ds(128 * j, 128), :] = block
                    cmat[j, pl.ds(128 * (c + h), 128), :] = jnp.transpose(block)
                    state[h] = running(part, block, *state[h])
        for h in range(2):
            close(rsend.at[0], c + h, *state[h])
        return carry

    def lse(mat, col, out, lo, hi):
        def step(i, carry):
            state = [(None, None)] * WIDE
            for r in range(PTS // 128):
                part = col[pl.ds(128 * r, 128), :]
                for h in range(WIDE):
                    state[h] = running(part, mat[WIDE * i + h, pl.ds(128 * r, 128), :], *state[h])
            for h in range(WIDE):
                close(out, WIDE * i + h, *state[h])
            return carry

        lax.fori_loop(lo // WIDE, hi // WIDE, step, 0)

    def lse_part(mat, col, out, half):
        def step(i, carry):
            tiles = [WIDE * i + h for h in range(WIDE)]
            state = [(kept[c, 0], kept[c, 1]) if half else (None, None) for c in tiles]
            for r in range(8 * half, 8 * half + 8):
                part = col[pl.ds(128 * r, 128), :]
                for h in range(WIDE):
                    state[h] = running(part, mat[tiles[h], pl.ds(128 * r, 128), :], *state[h])
            for h in range(WIDE):
                if half:
                    close(out, tiles[h], *state[h])
                else:
                    kept[tiles[h], 0] = state[h][0]
                    kept[tiles[h], 1] = state[h][1]
            return carry

        lax.fori_loop(0, TILES // WIDE, step, 0)

    def merge(parts):
        top = tree(jnp.maximum, parts)
        return top + jnp.log2(tree(jnp.add, [jnp.exp2(part - top) for part in parts]))

    for i, n in enumerate(LINE):
        got = tpeer(16 - 4 * n)
        done(sp.at[got], spsem.at[i, 1])
        for m in LINE:
            push(sp.at[got], sp.at[got], spsem.at[3], {"tgt": tpeer(m)})
        piece = tp.at[pl.ds(speer(8 - 2 * n) * 2, 2)]
        done(piece, tpsem.at[i, 1])
        push(piece, piece, tpsem.at[3], {"src": speer(1)})
        piece = ys.at[pl.ds(speer(8 - 2 * n) * 2, 2)]
        done(piece, ysem.at[i, 1])
        push(piece, piece, ysem.at[4], {"src": speer(1)})
        done(xs.at[got], xsem.at[i, 1])
        for m in LINE:
            half = xs.at[got, pl.ds(0, 64)]
            push(half, half, xsem.at[6 + i], {"tgt": tpeer(m)})
        got = tpeer(4 - n)
        done(xs.at[got], xsem.at[3 + i, 1])
        for m in LINE:
            half = xs.at[got, pl.ds(64, 64)]
            push(half, half, xsem.at[6 + LINE.index(m)], {"tgt": tpeer(4 * m)})
    def rows_of(ref, r):
        return jnp.concatenate([ref[t, r : r + 1, :] for t in range(TILES)], axis=0)

    done(tp.at[pl.ds(0, 8)], tpsem.at[3, 1])
    g, lb, yh = rows_of(tp, 0), rows_of(tp, 1), rows_of(tp, 2)
    lb = lb + tdead
    spread(lb + SCALE * (g - yh), gb)
    done(ys.at[pl.ds(0, 2)], ysem.at[3, 1])
    done(ys.at[pl.ds(0, 6)], ysem.at[4, 1])

    def send_rows(k, lo, hi):
        piece = pl.ds(lo, hi - lo)
        rrecv[k, pl.ds(tgt, 1), piece] = rsend[k, piece].reshape(1, hi - lo, 128)
        for d in FAR_T:
            push(rsend.at[k, piece], rrecv.at[k, tgt, piece], rsem.at[k, lo // 8], {"tgt": tpeer(d)})

    def send_cols(k):
        crecv[k, pl.ds(src, 1)] = csend[k].reshape(1, 16, 128)
        for d in FAR_S:
            push(csend.at[k], crecv.at[k, src], csem.at[k], {"src": speer(d)})

    def take_rows(k, f, half):
        piece = pl.ds(8 * half, 8)
        done(rrecv.at[k, pl.ds(0, 15), piece], rsem.at[k, half, 1])
        whole = merge([rrecv[k, i, piece] for i in range(NT)])
        return 0.5 * (f + (xh[8 * half : 8 * half + 8] - whole * (1.0 / SCALE)))

    def take_cols(k, g):
        done(crecv.at[k, pl.ds(0, 7)], csem.at[k, 1])
        return 0.5 * (g + (yh - merge([crecv[k, i] for i in range(NS)]) * (1.0 / SCALE)))

    lax.fori_loop(0, TILES // 2, first, 0)
    send_rows(0, 0, 8)
    send_rows(0, 8, 16)
    done(sp.at[pl.ds(0, 12)], spsem.at[3, 1])
    f, la, xh = rows_of(sp, 0), rows_of(sp, 1), rows_of(sp, 2)
    la = la + sdead
    spread(la + SCALE * (f - xh), fb)
    f = [f[0:8], f[8:16]]
    lse(cmat, fb, csend.at[0], 0, 16)
    send_cols(0)
    ytr[128:144, :] = jnp.ones((16, PTS), jnp.bfloat16)
    for t in range(TILES):
        ytr[0:128, pl.ds(128 * t, 128)] = jnp.transpose(ys[t].astype(jnp.float32)).astype(jnp.bfloat16)

    def row_half(k, g):
        g = take_cols(k - 1, g)
        spread(lb + SCALE * (g - yh), gb)
        for lo in (0, 8):
            lse(rmat, gb, rsend.at[k], lo, lo + 8)
            send_rows(k, lo, lo + 8)
        return g

    def col_half(k, f):
        f = list(f)
        for half in range(2):
            f[half] = take_rows(k - 1, f[half], half)
            at = slice(8 * half, 8 * half + 8)
            rows = la[at] + SCALE * (f[half] - xh[at])
            zero = jnp.zeros((8, 128), jnp.float32)
            spread(jnp.concatenate([zero, rows] if half else [rows, zero], axis=0), fb, (half,))
            lse_part(cmat, fb, csend.at[k], half)
        send_cols(k)
        return f

    for k in range(1, ITERS):
        if k % 2:
            f = col_half(k, f)
            g = row_half(k, g)
        else:
            g = row_half(k, g)
            f = col_half(k, f)
    g = take_cols(ITERS - 1, g)
    spread(lb + SCALE * (g - yh), gb)

    def project(i, carry):
        ds = [pick(i, ORDER[0::2]), pick(i, ORDER[1::2])]
        cs = [lax.rem(tx + lax.div(d, 4), 4) * 4 + lax.rem(ty + lax.rem(d, 4), 4) for d in ds]
        tops = [[], []]
        for r in range(16):
            part = gb[pl.ds(128 * r, 128), :]
            for h in range(2):
                v = rmat[cs[h], pl.ds(128 * r, 128), :] + part
                tops[h].append(fold(jnp.maximum, v))
        tops = [jnp.max(tree(jnp.maximum, t), axis=0, keepdims=True) for t in tops]
        for r in range(16):
            part = gb[pl.ds(128 * r, 128), :]
            for h in range(2):
                w = jnp.exp2((rmat[cs[h], pl.ds(128 * r, 128), :] + part) - tops[h])
                at = (pl.ds(128 * r, 128), slice(128 * h, 128 * h + 128))
                whi[at] = w.astype(jnp.bfloat16)
                wlo[at] = (w - whi[at].astype(jnp.float32)).astype(jnp.bfloat16)
        moved = jnp.dot(ytr[...], whi[...], preferred_element_type=jnp.float32) + jnp.dot(
            ytr[...], wlo[...], preferred_element_type=jnp.float32
        )
        r8 = iota((8, 128), 0)
        for h in range(2):
            block = moved[0:128, 128 * h : 128 * h + 128]
            most = jnp.max(fold(jnp.maximum, jnp.abs(block)), axis=0, keepdims=True)
            most = jnp.maximum(most, 1e-30)
            msg[ds[h]] = jnp.round(block * (32767.0 / most)).astype(jnp.int32).astype(jnp.int16)
            rows = (tops[h], moved[128:129, 128 * h : 128 * h + 128], most * (1.0 / 32767.0))
            stat[ds[h]] = tree(jnp.add, [jnp.where(r8 == n, jnp.broadcast_to(row, (8, 128)), 0.0) for n, row in enumerate(rows)])
        push(stat.at[ds[0]], srecv.at[ds[0]], ssem, {"tgt": cs[0]})
        push(msg.at[ds[0]], mrecv.at[ds[0]], msem, {"tgt": cs[0]})

        @pl.when(ds[1] > 0)
        def _():
            push(stat.at[ds[1]], srecv.at[ds[1]], ssem, {"tgt": cs[1]})
            push(msg.at[ds[1]], mrecv.at[ds[1]], msem, {"tgt": cs[1]})

        return carry

    lax.fori_loop(0, 8, project, 0)
    for half in range(2):
        fb[8 * half : 8 * half + 8, :] = take_rows(ITERS - 1, f[half], half)
    f_out[...] = from_lanes(fb[pl.ds(tgt, 1), :], 16)
    gb[0:16, :] = g
    g_out[...] = from_lanes(gb[pl.ds(src * 2, 2), :], 32)
    mrecv[0] = msg[0]
    srecv[0] = stat[0]
    done(srecv.at[pl.ds(1, 15)], ssem.at[1])
    tops = [srecv[d, 0:1, :] for d in range(16)]
    top = tree(jnp.maximum, tops)
    scales = [jnp.exp2(t - top) for t in tops]
    inv = 1.0 / tree(jnp.add, [scales[d] * srecv[d, 1:2, :] for d in range(16)])
    scales = [scales[d] * srecv[d, 2:3, :] * inv for d in range(16)]
    done(mrecv.at[pl.ds(1, 15)], msem.at[1])
    moved = tree(jnp.add, [scales[d] * mrecv[d].astype(jnp.int32).astype(jnp.float32) for d in range(16)])
    img_out[...] = jnp.transpose(moved)

    for i in range(6):
        done(xs.at[0], xsem.at[i, 0])
    for i in range(3):
        done(xs.at[pl.ds(0, 3)], xsem.at[6 + i, 0])
    for i in range(4):
        done(ys.at[pl.ds(0, 2)], ysem.at[i, 0])
    done(ys.at[pl.ds(0, 6)], ysem.at[4, 0])
    for i in range(3):
        done(sp.at[0], spsem.at[i, 0])
        done(tp.at[pl.ds(0, 2)], tpsem.at[i, 0])
    done(sp.at[pl.ds(0, 12)], spsem.at[3, 0])
    done(tp.at[pl.ds(0, 8)], tpsem.at[3, 0])
    for k in range(ITERS):
        for half in range(2):
            done(rrecv.at[k, pl.ds(0, 15), pl.ds(8 * half, 8)], rsem.at[k, half, 0])
        done(crecv.at[k, pl.ds(0, 7)], csem.at[k, 0])
    done(mrecv.at[pl.ds(1, 15)], msem.at[0])
    done(srecv.at[pl.ds(1, 15)], ssem.at[0])


def on_device(src_points, tgt_points, src_mass, tgt_mass, src_potential, tgt_potential, src_counts, tgt_counts, keep):
    f32, bf16 = jnp.float32, jnp.bfloat16
    vmem = pl.BlockSpec(memory_space=pltpu.VMEM)
    smem = pl.BlockSpec(memory_space=pltpu.SMEM)
    dma = pltpu.SemaphoreType.DMA
    images, f, g = pl.pallas_call(
        kernel,
        out_shape=(
            jax.ShapeDtypeStruct((128, 128), f32),
            jax.ShapeDtypeStruct((8, 16), f32),
            jax.ShapeDtypeStruct((8, 32), f32),
        ),
        in_specs=[smem] * 3 + [vmem] * 6,
        out_specs=(vmem, vmem, vmem),
        scratch_shapes=[
            pltpu.VMEM((16, 128, 128), bf16),
            pltpu.VMEM((16, 128, 128), bf16),
            pltpu.VMEM((16, 8, 128), f32),
            pltpu.VMEM((16, 8, 128), f32),
            pltpu.VMEM((144, PTS), bf16),
            pltpu.VMEM((16, PTS, 128), f32),
            pltpu.VMEM((16, PTS, 128), f32),
            pltpu.VMEM((2, PTS, 128), f32),
            pltpu.VMEM((PTS, 128), f32),
            pltpu.VMEM((PTS, 128), f32),
            pltpu.VMEM((48, PTS), bf16),
            pltpu.VMEM((256, 128), f32),
            pltpu.VMEM((PTS, 256), bf16),
            pltpu.VMEM((PTS, 256), bf16),
            pltpu.VMEM((8, 128), f32),
            pltpu.VMEM((2, 8, 128), f32),
            pltpu.VMEM((ITERS, 16, 128), f32),
            pltpu.VMEM((ITERS, 16, 16, 128), f32),
            pltpu.VMEM((ITERS, 16, 128), f32),
            pltpu.VMEM((ITERS, 8, 16, 128), f32),
            pltpu.VMEM((16, 128, 128), jnp.int16),
            pltpu.VMEM((16, 128, 128), jnp.int16),
            pltpu.VMEM((16, 8, 128), f32),
            pltpu.VMEM((16, 8, 128), f32),
            dma((9, 2)),
            dma((4, 2)),
            dma((5, 2)),
            dma((4, 2)),
            dma((ITERS, 2, 2)),
            dma((ITERS, 2)),
            dma((2,)),
            dma((2,)),
            pltpu.VMEM((TILES, 2, 8, 128), f32),
        ],
        compiler_params=pltpu.CompilerParams(
            collective_id=0, has_side_effects=True, vmem_limit_bytes=60 * 1024 * 1024
        ),
        name="sinkhorn",
    )(
        src_counts,
        tgt_counts,
        keep,
        src_points.reshape(128, 128),
        tgt_points.reshape(2, 128, 128),
        src_mass,
        tgt_mass,
        src_potential,
        tgt_potential,
    )
    return images.reshape(8, 16, 128), f, g


def solution(mesh):
    return jax.shard_map(
        on_device,
        mesh=mesh,
        in_specs=(
            P("src", "tgt", None),
            P("tgt", "src", None),
            P("src", "tgt"),
            P("tgt", "src"),
            P("src", "tgt"),
            P("tgt", "src"),
            P("src"),
            P("tgt"),
            P("src", "tgt"),
        ),
        out_specs=(P("src", "tgt", None), P("src", "tgt"), P("tgt", "src")),
        check_vma=False,
    )
```

```python
import math

import jax
import jax.numpy as jnp
from jax import lax
from jax.experimental import pallas as pl
from jax.experimental.pallas import tpu as pltpu
from jax.sharding import PartitionSpec as P

ITERS = 4
EPSILON = 0.1
NEG = -1e30
SCALE = math.log2(math.e) / EPSILON
MESH = pl.DeviceIdType.MESH

NT, NS = 16, 8
PTS = 2048
TILES = 16
WIDE = 4
FAR_T = sorted(range(1, NT), key=lambda d: -(min(d // 4, 4 - d // 4) + min(d % 4, 4 - d % 4)))
LINE = (1, 3, 2)
ORDER = FAR_T + [0]
FAR_S = sorted(range(1, NS), key=lambda d: -(2 * min(d // 2, 4 - d // 2) + d % 2))


def iota(shape, dim):
    return lax.broadcasted_iota(jnp.int32, shape, dim)


def pick(i, values):
    return sum(jnp.where(i == n, v, 0) for n, v in enumerate(values))


def tree(op, parts):
    parts = list(parts)
    while len(parts) > 1:
        parts = [op(parts[i], parts[i + 1]) if i + 1 < len(parts) else parts[i] for i in range(0, len(parts), 2)]
    return parts[0]


def fold(op, block):
    return tree(op, [block[8 * i : 8 * i + 8, :] for i in range(block.shape[0] // 8)])


def to_lanes(block):
    n = block.shape[1]
    put = (iota((n, 8 * n), 1) % n == iota((n, 8 * n), 0)).astype(jnp.bfloat16)
    wide = jnp.dot(block, put, preferred_element_type=jnp.float32)
    own = iota((8, 8 * n), 1) // n == iota((8, 8 * n), 0)
    return jnp.sum(jnp.where(own, wide, 0.0), axis=0, keepdims=True)


def thirds(wide):
    high = wide.astype(jnp.bfloat16)
    rest = wide - high.astype(jnp.float32)
    mid = rest.astype(jnp.bfloat16)
    return high, mid, (rest - mid.astype(jnp.float32)).astype(jnp.bfloat16)


def from_lanes(rows, n):
    per = 128 // n
    home, lane = iota((8, 128), 0), iota((8, 128), 1)
    wide = jnp.zeros((8, 128), jnp.float32)
    for h in range(rows.shape[0]):
        wide = jnp.where(home == h * per + lane // n, jnp.broadcast_to(rows[h : h + 1, :], (8, 128)), wide)
    put = (iota((128, n), 0) % n == iota((128, n), 1)).astype(jnp.bfloat16)
    parts = [jnp.dot(part, put, preferred_element_type=jnp.float32) for part in thirds(wide)]
    return parts[0] + parts[1] + parts[2]


def half_norm(points):
    wide = points.astype(jnp.float32)
    square = wide * wide
    high = square.astype(jnp.bfloat16)
    low = (square - high.astype(jnp.float32)).astype(jnp.bfloat16)
    ones = jnp.ones((8, 128), jnp.bfloat16)
    dims = (((1,), (1,)), ((), ()))
    total = lax.dot_general(ones, high, dims, preferred_element_type=jnp.float32) + lax.dot_general(
        ones, low, dims, preferred_element_type=jnp.float32
    )
    return 0.5 * total[0:1, :]


def kernel(
    scnt, tcnt, keep, x_in, y_in, a_in, b_in, f_in, g_in, img_out, f_out, g_out,
    xs, ys, sp, tp, ytr, cmat, rmat, vbuf, fb, gb, sel, pt, whi, wlo, fl, gl,
    rsend, rrecv, csend, crecv, msg, mrecv, stat, srecv,
    xsem, spsem, ysem, tpsem, rsem, csem, msem, ssem, kept,
):
    src = lax.axis_index("src")
    tgt = lax.axis_index("tgt")
    sz, sc = lax.div(src, 2), lax.rem(src, 2)
    tx, ty = lax.div(tgt, 4), lax.rem(tgt, 4)

    def tpeer(d):
        return lax.rem(tx + d // 4, 4) * 4 + lax.rem(ty + d % 4, 4)

    def speer(d):
        return lax.rem(sz + d // 2, 4) * 2 + lax.rem(sc + d % 2, 2)

    barrier = pltpu.get_barrier_semaphore()
    for n in LINE:
        pl.semaphore_signal(barrier, inc=1, device_id={"tgt": tpeer(4 * n)}, device_id_type=MESH)
        pl.semaphore_signal(barrier, inc=1, device_id={"tgt": tpeer(n)}, device_id_type=MESH)
        pl.semaphore_signal(barrier, inc=1, device_id={"src": speer(2 * n)}, device_id_type=MESH)
    pl.semaphore_signal(barrier, inc=1, device_id={"src": speer(1)}, device_id_type=MESH)

    def push(source, dest, sem, device):
        pltpu.make_async_remote_copy(
            src_ref=source, dst_ref=dest, send_sem=sem.at[0], recv_sem=sem.at[1], device_id=device, device_id_type=MESH
        ).start()

    def done(ref, sem):
        pltpu.make_async_copy(ref, ref, sem).wait()

    lane = iota((1, 128), 1)
    xs[pl.ds(tgt, 1)] = x_in[...].reshape(1, 128, 128)
    ys[pl.ds(src * 2, 2)] = y_in[...].reshape(2, 128, 128)
    fl[...] = jnp.zeros((8, 128), jnp.float32)
    gl[...] = jnp.zeros((2, 8, 128), jnp.float32)
    fl[0:1, :] = to_lanes(f_in[...])
    fl[1:2, :] = jnp.log2(to_lanes(a_in[...]))
    fl[2:3, :] = half_norm(x_in[...])
    tgt_rows = (to_lanes(g_in[...]), jnp.log2(to_lanes(b_in[...])), half_norm(y_in[...].reshape(256, 128)))
    for r, row in enumerate(tgt_rows):
        for h in range(2):
            gl[h, r : r + 1, :] = row[:, 128 * h : 128 * h + 128]
    sp[pl.ds(tgt, 1)] = fl[...].reshape(1, 8, 128)
    tp[pl.ds(src * 2, 2)] = gl[...]

    pl.semaphore_wait(barrier, 10)
    mine_y = pl.ds(src * 2, 2)
    for i, n in enumerate(LINE):
        push(fl, sp.at[tgt], spsem.at[i], {"tgt": tpeer(4 * n)})
        push(fl, sp.at[tgt], spsem.at[3], {"tgt": tpeer(n)})
        push(gl, tp.at[mine_y], tpsem.at[i], {"src": speer(2 * n)})
        push(x_in, xs.at[tgt], xsem.at[i], {"tgt": tpeer(4 * n)})
        push(x_in, xs.at[tgt], xsem.at[3 + i], {"tgt": tpeer(n)})
        push(y_in, ys.at[mine_y], ysem.at[i], {"src": speer(2 * n)})
    push(gl, tp.at[mine_y], tpsem.at[3], {"src": speer(1)})
    push(y_in, ys.at[mine_y], ysem.at[3], {"src": speer(1)})

    for q in range(8):
        row = jnp.zeros((1, 128), jnp.float32)
        for p in range(8):
            pen = jnp.where(keep[p, q] > 0, 0.0, NEG)
            row = jnp.where(lane // 16 == p, pen, row)
        pt[pl.ds(32 * q, 32), :] = jnp.broadcast_to(row, (32, 128))
    r16, l16 = iota((16, 128), 0), iota((16, 128), 1)
    sdead = jnp.zeros((16, 128), jnp.float32)
    tdead = jnp.zeros((16, 128), jnp.float32)
    for p in range(8):
        sdead = jnp.where((l16 // 16 == p) & (r16 * 16 + l16 % 16 >= scnt[p]), NEG, sdead)
        tdead = jnp.where(((r16 % 2) * 4 + l16 // 32 == p) & ((r16 // 2) * 32 + l16 % 32 >= tcnt[p]), NEG, tdead)
    sel[...] = (iota((48, PTS), 0) % 16 == iota((48, PTS), 1) // 128).astype(jnp.bfloat16)

    def spread(rows, dest, halves=(0, 1)):
        parts = jnp.concatenate(thirds(rows), axis=0)
        for half in halves:
            wide = lax.dot_general(
                parts, sel[:, 1024 * half : 1024 * half + 1024], (((0,), (0,)), ((), ())), preferred_element_type=jnp.float32
            )
            for t in range(8):
                dest[pl.ds(1024 * half + 128 * t, 128), :] = wide[:, 128 * t : 128 * t + 128]

    def running(part, block, top, total):
        vs = [block[8 * n : 8 * n + 8, :] + part[8 * n : 8 * n + 8, :] for n in range(16)]
        new = tree(jnp.maximum, vs if top is None else vs + [top])
        more = tree(jnp.add, [jnp.exp2(u - new) for u in vs])
        return new, more if top is None else total * jnp.exp2(top - new) + more

    def close(out, c, top8, total8):
        top = jnp.max(top8, axis=0, keepdims=True)
        total = jnp.sum(total8 * jnp.exp2(top8 - top), axis=0, keepdims=True)
        out[pl.ds(c, 1), :] = top + jnp.log2(total)

    def first(i, carry):
        k = i // 2
        dx = k + (k // 2) * (1 - 2 * (k % 2))

        @pl.when((i % 2 == 0) & (i > 0))
        def _():
            done(xs.at[pl.ds(0, 3)], xsem.at[5 + k, 1])

        c = lax.rem(tx + 4 - dx, 4) * 4 + 2 * (i % 2)
        two = jnp.transpose(xs[pl.ds(c, 2)].reshape(256, 128).astype(jnp.float32)).astype(jnp.bfloat16)
        state = [(None, None)] * 2
        for r in range(8):
            prod = jnp.dot(ys[2 * r : 2 * r + 2].reshape(256, 128), two, preferred_element_type=jnp.float32)
            for v in range(2):
                j = 2 * r + v
                part = gb[pl.ds(128 * j, 128), :]
                for h in range(2):
                    block = SCALE * prod[128 * v : 128 * v + 128, 128 * h : 128 * h + 128] + pt[128 * v : 128 * v + 128, :]
                    rmat[c + h, pl.ds(128 * j, 128), :] = block
                    if v == 0:
                        cmat[j, pl.ds(128 * (c + h), 128), :] = jnp.transpose(block)
                    state[h] = running(part, block, *state[h])
        for h in range(2):
            close(rsend.at[0], c + h, *state[h])
        return carry

    def lse(mat, col, out, lo, hi):
        def step(i, carry):
            state = [(None, None)] * WIDE
            for r in range(PTS // 128):
                part = col[pl.ds(128 * r, 128), :]
                for h in range(WIDE):
                    state[h] = running(part, mat[WIDE * i + h, pl.ds(128 * r, 128), :], *state[h])
            for h in range(WIDE):
                close(out, WIDE * i + h, *state[h])
            return carry

        lax.fori_loop(lo // WIDE, hi // WIDE, step, 0)

    def first_cols(i, carry):
        state = [(None, None)] * WIDE
        for r in range(TILES):
            part = fb[pl.ds(128 * r, 128), :]
            for h in range(WIDE):
                c = WIDE * i + h
                if h % 2:
                    block = jnp.transpose(rmat[r, pl.ds(128 * c, 128), :])
                    cmat[c, pl.ds(128 * r, 128), :] = block
                else:
                    block = cmat[c, pl.ds(128 * r, 128), :]
                state[h] = running(part, block, *state[h])
        for h in range(WIDE):
            close(csend.at[0], WIDE * i + h, *state[h])
        return carry

    def lse_part(mat, col, out, half):
        def step(i, carry):
            tiles = [WIDE * i + h for h in range(WIDE)]
            state = [(kept[c, 0], kept[c, 1]) if half else (None, None) for c in tiles]
            for r in range(8 * half, 8 * half + 8):
                part = col[pl.ds(128 * r, 128), :]
                for h in range(WIDE):
                    state[h] = running(part, mat[tiles[h], pl.ds(128 * r, 128), :], *state[h])
            for h in range(WIDE):
                if half:
                    close(out, tiles[h], *state[h])
                else:
                    kept[tiles[h], 0] = state[h][0]
                    kept[tiles[h], 1] = state[h][1]
            return carry

        lax.fori_loop(0, TILES // WIDE, step, 0)

    def merge(parts):
        top = tree(jnp.maximum, parts)
        return top + jnp.log2(tree(jnp.add, [jnp.exp2(part - top) for part in parts]))

    for i, n in enumerate(LINE):
        got = tpeer(16 - 4 * n)
        done(sp.at[got], spsem.at[i, 1])
        for m in LINE:
            push(sp.at[got], sp.at[got], spsem.at[3], {"tgt": tpeer(m)})
        piece = tp.at[pl.ds(speer(8 - 2 * n) * 2, 2)]
        done(piece, tpsem.at[i, 1])
        push(piece, piece, tpsem.at[3], {"src": speer(1)})
        piece = ys.at[pl.ds(speer(8 - 2 * n) * 2, 2)]
        done(piece, ysem.at[i, 1])
        push(piece, piece, ysem.at[4], {"src": speer(1)})
        done(xs.at[got], xsem.at[i, 1])
        for m in LINE:
            half = xs.at[got, pl.ds(0, 64)]
            push(half, half, xsem.at[6 + i], {"tgt": tpeer(m)})
        got = tpeer(4 - n)
        done(xs.at[got], xsem.at[3 + i, 1])
        for m in LINE:
            half = xs.at[got, pl.ds(64, 64)]
            push(half, half, xsem.at[6 + LINE.index(m)], {"tgt": tpeer(4 * m)})
    def rows_of(ref, r):
        return jnp.concatenate([ref[t, r : r + 1, :] for t in range(TILES)], axis=0)

    done(tp.at[pl.ds(0, 8)], tpsem.at[3, 1])
    g, lb, yh = rows_of(tp, 0), rows_of(tp, 1), rows_of(tp, 2)
    lb = lb + tdead
    spread(lb + SCALE * (g - yh), gb)
    done(ys.at[pl.ds(0, 2)], ysem.at[3, 1])
    done(ys.at[pl.ds(0, 6)], ysem.at[4, 1])

    def send_rows(k, lo, hi):
        piece = pl.ds(lo, hi - lo)
        rrecv[k, pl.ds(tgt, 1), piece] = rsend[k, piece].reshape(1, hi - lo, 128)
        for d in FAR_T:
            push(rsend.at[k, piece], rrecv.at[k, tgt, piece], rsem.at[k, lo // 8], {"tgt": tpeer(d)})

    def send_cols(k):
        crecv[k, pl.ds(src, 1)] = csend[k].reshape(1, 16, 128)
        for d in FAR_S:
            push(csend.at[k], crecv.at[k, src], csem.at[k], {"src": speer(d)})

    def take_rows(k, f, half):
        piece = pl.ds(8 * half, 8)
        done(rrecv.at[k, pl.ds(0, 15), piece], rsem.at[k, half, 1])
        whole = merge([rrecv[k, i, piece] for i in range(NT)])
        return 0.5 * (f + (xh[8 * half : 8 * half + 8] - whole * (1.0 / SCALE)))

    def take_cols(k, g):
        done(crecv.at[k, pl.ds(0, 7)], csem.at[k, 1])
        return 0.5 * (g + (yh - merge([crecv[k, i] for i in range(NS)]) * (1.0 / SCALE)))

    lax.fori_loop(0, TILES // 2, first, 0)
    send_rows(0, 0, 8)
    send_rows(0, 8, 16)
    done(sp.at[pl.ds(0, 12)], spsem.at[3, 1])
    f, la, xh = rows_of(sp, 0), rows_of(sp, 1), rows_of(sp, 2)
    la = la + sdead
    spread(la + SCALE * (f - xh), fb)
    f = [f[0:8], f[8:16]]
    lax.fori_loop(0, TILES // WIDE, first_cols, 0)
    send_cols(0)
    ytr[128:144, :] = jnp.ones((16, PTS), jnp.bfloat16)
    for t in range(TILES):
        ytr[0:128, pl.ds(128 * t, 128)] = jnp.transpose(ys[t].astype(jnp.float32)).astype(jnp.bfloat16)

    def row_half(k, g):
        g = take_cols(k - 1, g)
        spread(lb + SCALE * (g - yh), gb)
        for lo in (0, 8):
            lse(rmat, gb, rsend.at[k], lo, lo + 8)
            send_rows(k, lo, lo + 8)
        return g

    def col_half(k, f):
        f = [take_rows(k - 1, f[half], half) for half in range(2)]
        spread(la + SCALE * (jnp.concatenate(f, axis=0) - xh), fb)
        lse(cmat, fb, csend.at[k], 0, 16)
        send_cols(k)
        return f

    for k in range(1, ITERS):
        if k % 2:
            f = col_half(k, f)
            g = row_half(k, g)
        else:
            g = row_half(k, g)
            f = col_half(k, f)
    g = take_cols(ITERS - 1, g)
    spread(lb + SCALE * (g - yh), gb)

    def project(i, carry):
        ds = [pick(i, ORDER[0::2]), pick(i, ORDER[1::2])]
        cs = [lax.rem(tx + lax.div(d, 4), 4) * 4 + lax.rem(ty + lax.rem(d, 4), 4) for d in ds]
        tops = [[], []]
        for r in range(16):
            part = gb[pl.ds(128 * r, 128), :]
            for h in range(2):
                v = rmat[cs[h], pl.ds(128 * r, 128), :] + part
                tops[h].append(fold(jnp.maximum, v))
        tops = [jnp.max(tree(jnp.maximum, t), axis=0, keepdims=True) for t in tops]
        for r in range(16):
            part = gb[pl.ds(128 * r, 128), :]
            for h in range(2):
                w = jnp.exp2((rmat[cs[h], pl.ds(128 * r, 128), :] + part) - tops[h])
                at = (pl.ds(128 * r, 128), slice(128 * h, 128 * h + 128))
                whi[at] = w.astype(jnp.bfloat16)
                wlo[at] = (w - whi[at].astype(jnp.float32)).astype(jnp.bfloat16)
        moved = jnp.dot(ytr[...], whi[...], preferred_element_type=jnp.float32) + jnp.dot(
            ytr[...], wlo[...], preferred_element_type=jnp.float32
        )
        r8 = iota((8, 128), 0)
        for h in range(2):
            block = moved[0:128, 128 * h : 128 * h + 128]
            most = jnp.max(fold(jnp.maximum, jnp.abs(block)), axis=0, keepdims=True)
            most = jnp.maximum(most, 1e-30)
            msg[ds[h]] = jnp.round(block * (32767.0 / most)).astype(jnp.int32).astype(jnp.int16)
            rows = (tops[h], moved[128:129, 128 * h : 128 * h + 128], most * (1.0 / 32767.0))
            stat[ds[h]] = tree(jnp.add, [jnp.where(r8 == n, jnp.broadcast_to(row, (8, 128)), 0.0) for n, row in enumerate(rows)])
        push(stat.at[ds[0]], srecv.at[ds[0]], ssem, {"tgt": cs[0]})
        push(msg.at[ds[0]], mrecv.at[ds[0]], msem, {"tgt": cs[0]})

        @pl.when(ds[1] > 0)
        def _():
            push(stat.at[ds[1]], srecv.at[ds[1]], ssem, {"tgt": cs[1]})
            push(msg.at[ds[1]], mrecv.at[ds[1]], msem, {"tgt": cs[1]})

        return carry

    lax.fori_loop(0, 8, project, 0)
    for half in range(2):
        fb[8 * half : 8 * half + 8, :] = take_rows(ITERS - 1, f[half], half)
    f_out[...] = from_lanes(fb[pl.ds(tgt, 1), :], 16)
    gb[0:16, :] = g
    g_out[...] = from_lanes(gb[pl.ds(src * 2, 2), :], 32)
    mrecv[0] = msg[0]
    srecv[0] = stat[0]
    done(srecv.at[pl.ds(1, 15)], ssem.at[1])
    tops = [srecv[d, 0:1, :] for d in range(16)]
    top = tree(jnp.maximum, tops)
    scales = [jnp.exp2(t - top) for t in tops]
    inv = 1.0 / tree(jnp.add, [scales[d] * srecv[d, 1:2, :] for d in range(16)])
    scales = [scales[d] * srecv[d, 2:3, :] * inv for d in range(16)]
    done(mrecv.at[pl.ds(1, 15)], msem.at[1])
    moved = tree(jnp.add, [scales[d] * mrecv[d].astype(jnp.int32).astype(jnp.float32) for d in range(16)])
    img_out[...] = jnp.transpose(moved)

    for i in range(6):
        done(xs.at[0], xsem.at[i, 0])
    for i in range(3):
        done(xs.at[pl.ds(0, 3)], xsem.at[6 + i, 0])
    for i in range(4):
        done(ys.at[pl.ds(0, 2)], ysem.at[i, 0])
    done(ys.at[pl.ds(0, 6)], ysem.at[4, 0])
    for i in range(3):
        done(sp.at[0], spsem.at[i, 0])
        done(tp.at[pl.ds(0, 2)], tpsem.at[i, 0])
    done(sp.at[pl.ds(0, 12)], spsem.at[3, 0])
    done(tp.at[pl.ds(0, 8)], tpsem.at[3, 0])
    for k in range(ITERS):
        for half in range(2):
            done(rrecv.at[k, pl.ds(0, 15), pl.ds(8 * half, 8)], rsem.at[k, half, 0])
        done(crecv.at[k, pl.ds(0, 7)], csem.at[k, 0])
    done(mrecv.at[pl.ds(1, 15)], msem.at[0])
    done(srecv.at[pl.ds(1, 15)], ssem.at[0])


def on_device(src_points, tgt_points, src_mass, tgt_mass, src_potential, tgt_potential, src_counts, tgt_counts, keep):
    f32, bf16 = jnp.float32, jnp.bfloat16
    vmem = pl.BlockSpec(memory_space=pltpu.VMEM)
    smem = pl.BlockSpec(memory_space=pltpu.SMEM)
    dma = pltpu.SemaphoreType.DMA
    images, f, g = pl.pallas_call(
        kernel,
        out_shape=(
            jax.ShapeDtypeStruct((128, 128), f32),
            jax.ShapeDtypeStruct((8, 16), f32),
            jax.ShapeDtypeStruct((8, 32), f32),
        ),
        in_specs=[smem] * 3 + [vmem] * 6,
        out_specs=(vmem, vmem, vmem),
        scratch_shapes=[
            pltpu.VMEM((16, 128, 128), bf16),
            pltpu.VMEM((16, 128, 128), bf16),
            pltpu.VMEM((16, 8, 128), f32),
            pltpu.VMEM((16, 8, 128), f32),
            pltpu.VMEM((144, PTS), bf16),
            pltpu.VMEM((16, PTS, 128), f32),
            pltpu.VMEM((16, PTS, 128), f32),
            pltpu.VMEM((2, PTS, 128), f32),
            pltpu.VMEM((PTS, 128), f32),
            pltpu.VMEM((PTS, 128), f32),
            pltpu.VMEM((48, PTS), bf16),
            pltpu.VMEM((256, 128), f32),
            pltpu.VMEM((PTS, 256), bf16),
            pltpu.VMEM((PTS, 256), bf16),
            pltpu.VMEM((8, 128), f32),
            pltpu.VMEM((2, 8, 128), f32),
            pltpu.VMEM((ITERS, 16, 128), f32),
            pltpu.VMEM((ITERS, 16, 16, 128), f32),
            pltpu.VMEM((ITERS, 16, 128), f32),
            pltpu.VMEM((ITERS, 8, 16, 128), f32),
            pltpu.VMEM((16, 128, 128), jnp.int16),
            pltpu.VMEM((16, 128, 128), jnp.int16),
            pltpu.VMEM((16, 8, 128), f32),
            pltpu.VMEM((16, 8, 128), f32),
            dma((9, 2)),
            dma((4, 2)),
            dma((5, 2)),
            dma((4, 2)),
            dma((ITERS, 2, 2)),
            dma((ITERS, 2)),
            dma((2,)),
            dma((2,)),
            pltpu.VMEM((TILES, 2, 8, 128), f32),
        ],
        compiler_params=pltpu.CompilerParams(
            collective_id=0, has_side_effects=True, vmem_limit_bytes=60 * 1024 * 1024
        ),
        name="sinkhorn",
    )(
        src_counts,
        tgt_counts,
        keep,
        src_points.reshape(128, 128),
        tgt_points.reshape(2, 128, 128),
        src_mass,
        tgt_mass,
        src_potential,
        tgt_potential,
    )
    return images.reshape(8, 16, 128), f, g


def solution(mesh):
    return jax.shard_map(
        on_device,
        mesh=mesh,
        in_specs=(
            P("src", "tgt", None),
            P("tgt", "src", None),
            P("src", "tgt"),
            P("tgt", "src"),
            P("src", "tgt"),
            P("tgt", "src"),
            P("src"),
            P("tgt"),
            P("src", "tgt"),
        ),
        out_specs=(P("src", "tgt", None), P("src", "tgt"), P("tgt", "src")),
        check_vma=False,
    )
```
